32 devices in a mesh: gz: 4 (over y, x), gy: 2 (over core), gx: 4 (over z).
Axes of the slice: x: 2, y: 2, z: 4, core: 2. Of those that a mesh axis runs over, the one named last changes fastest.
Arguments:
- vectors: bfloat16 [4, 2, 4, 4, 24, 2, 4, 3, 256], P('gz', 'gy', 'gx'), may hold values from -6 to 6
- links: bfloat16 [4, 2, 4, 4, 4, 2, 3, 3, 256], P('gz', 'gy', 'gx'), may hold values from -2.5 to 2.5
- site_term: bfloat16 [4, 2, 4, 4, 2, 2, 6, 6, 256], P('gz', 'gy', 'gx'), may hold values from -3 to 3, as said below
- owner: int32 [4, 2, 4, 4], replicated, may hold values from 0 to 15, as said below
- coarse_rhs: bfloat16 [4, 2, 4, 4, 2, 24], P('gz', 'gy', 'gx'), may hold values from -50 to 50
Outputs:
- coarse_operator: bfloat16 [16, 32, 9, 2, 576], P(('gz', 'gx'))
- coarse_solution: float32 [16, 32, 2, 24], P(('gz', 'gx'))
The draws below stay inside these ranges and needn't reach their ends.
Inputs may be any that keep to these rules, and one draw needn't show every extreme that they name: Within each block of 4 aggregates with the same z, y, x no owner appears more than 1 times, and one owner appears exactly 1 times in every block. `site_term`: each chirality block is Hermitian.
All inputs are finite; a program needn't handle non-finite values.
Results may differ from the reference program's by a relative error of at most 0.009.
Values may be sent and summed in bfloat16 or wider, within the bound.
A program may use at most 128 MiB of HBM per device.

```python
import math
import jax
import jax.numpy as jnp
import numpy as np
from jax import lax

NV = 24
AT = 4
ITERS = 4
PAIR = 1
CAP = 32
N_GZ = 4
N_GY = 2
N_GX = 4


def draw_site_term(key, part):
    shape_all = (N_GZ, N_GY, N_GX, AT, 2, 2, 6, 6, 256)
    raw_draw = jnp.clip(jax.random.normal(key, shape_all, jnp.float32) * 0.5, -3.0, 3.0)
    real_part = raw_draw[:, :, :, :, :, 0]
    imag_part = raw_draw[:, :, :, :, :, 1]
    herm_re = (real_part + jnp.swapaxes(real_part, -3, -2)) * 0.5
    herm_im = (imag_part - jnp.swapaxes(imag_part, -3, -2)) * 0.5
    return jnp.stack([herm_re, herm_im], axis=5).astype(jnp.bfloat16)


def draw_coarse_rhs(key, part):
    key_base = jax.random.fold_in(key, 11)
    key_scale = jax.random.fold_in(key, 12)
    shape_all = (N_GZ, N_GY, N_GX, AT, 2, NV)
    base_draw = jnp.clip(jax.random.normal(key_base, shape_all, jnp.float32), -5.0, 5.0)
    row_scale = jnp.exp(jax.random.uniform(key_scale, (N_GZ, N_GY, N_GX, AT, 1, 1), jnp.float32, 0.0, math.log(10.0)))
    return (base_draw * row_scale).astype(jnp.bfloat16)


def draw_owner(key, part):
    block_count = N_GZ * N_GY * N_GX
    owners_count = N_GZ * N_GX
    label_count = (owners_count - 1) * PAIR
    key_full = jax.random.fold_in(key, 21)
    key_pick = jax.random.fold_in(key, 22)
    key_order = jax.random.fold_in(key, 23)
    full_owner = jax.random.randint(key_full, (), 0, owners_count, dtype=jnp.int32)
    labels = jnp.arange(label_count, dtype=jnp.int32) // PAIR
    others = labels + (labels >= full_owner).astype(jnp.int32)
    scores = jax.random.randint(key_pick, (block_count, label_count), 0, 1048576, dtype=jnp.int32) * label_count + jnp.arange(label_count, dtype=jnp.int32)
    order = jnp.argsort(scores, axis=1)
    picked = others[order[:, :AT - PAIR]]
    filled = jnp.concatenate([jnp.full((block_count, PAIR), full_owner, jnp.int32), picked], axis=1)
    scores_two = jax.random.randint(key_order, (block_count, AT), 0, 1048576, dtype=jnp.int32) * AT + jnp.arange(AT, dtype=jnp.int32)
    positions = jnp.argsort(scores_two, axis=1)
    mixed = jnp.take_along_axis(filled, positions, axis=1)
    return mixed.reshape(N_GZ, N_GY, N_GX, AT).astype(jnp.int32)


def levels(own_key, shape, cuts, low, top_value):
    level, own = 1.0, jax.random.fold_in(own_key, 6)
    for dim, parts in cuts:
        steps = jnp.exp(jax.random.uniform(jax.random.fold_in(own, dim), (parts,), jnp.float32, low / len(cuts), top_value / len(cuts)))
        level = level * jnp.repeat(steps, shape[dim] // parts).reshape([-1 if axis == dim else 1 for axis in range(len(shape))])
    return level


def bell_draw(rng, shape, deviation, limit, cuts=(), kind=jnp.bfloat16):
    entries = jax.random.normal(rng, shape, jnp.float32) * deviation
    if len(cuts) > 0:
        entries = levels(rng, shape, cuts, -0.22, 0.18) * entries
    return jnp.clip(entries, min=-limit, max=limit).astype(kind)


def setup_inputs(seed: int = 0) -> dict:
    arg_keys = jax.random.split(jax.random.key(seed), 6)
    vectors = bell_draw(arg_keys[0], (N_GZ, N_GY, N_GX, AT, NV, 2, 4, 3, 256), 1.0, 6.0, ((0, 4), (1, 2), (2, 4)))
    links = bell_draw(arg_keys[1], (N_GZ, N_GY, N_GX, AT, 4, 2, 3, 3, 256), 6 ** -0.5, 2.5, ((0, 4), (1, 2), (2, 4)))
    site_term = draw_site_term(jax.random.fold_in(arg_keys[5], 71), 0)
    owner = draw_owner(jax.random.fold_in(arg_keys[5], 71), 0)
    coarse_rhs = draw_coarse_rhs(jax.random.fold_in(arg_keys[5], 71), 0)
    return dict(vectors=vectors, links=links, site_term=site_term, owner=owner, coarse_rhs=coarse_rhs)


coarse_scale = 1.0 / 256.0
epsilon = 1e-06
site_strides = (64, 16, 4, 1)
roll_axes = (2, 1, 0, 3)

def face_table(stride, layer_index):
    position = np.arange(64)
    return position // stride * 4 * stride + position % stride + layer_index * stride

def take_sites(array_in, stride, layer_index):
    picks = jnp.asarray(face_table(stride, layer_index), dtype=jnp.int32)
    return jnp.take(array_in, picks, axis=-1)

def times_spin(direction, lower_part):
    real_zero = lower_part[..., 0, 0, :, :]
    real_one = lower_part[..., 0, 1, :, :]
    imag_zero = lower_part[..., 1, 0, :, :]
    imag_one = lower_part[..., 1, 1, :, :]
    if direction == 0:
        pieces = ((imag_one, imag_zero), (-real_one, -real_zero))
    elif direction == 1:
        pieces = ((-real_one, real_zero), (-imag_one, imag_zero))
    elif direction == 2:
        pieces = ((imag_zero, -imag_one), (-real_zero, real_one))
    else:
        return lower_part
    return jnp.stack([jnp.stack(pieces[0], -3), jnp.stack(pieces[1], -3)], -4)

def project(vectors, direction):
    spinor = vectors.astype(jnp.float32)
    upper_part = spinor[:, :, :, 0:2]
    lower_part = times_spin(direction, spinor[:, :, :, 2:4])
    return ((upper_part - lower_part).astype(jnp.bfloat16), (upper_part + lower_part).astype(jnp.bfloat16))

def transport(link_field, half_field, adjoint):
    link_field = link_field.astype(jnp.float32)
    half_field = half_field.astype(jnp.float32)
    link_re = link_field[:, 0][:, None, None]
    link_im = link_field[:, 1][:, None, None]
    half_re = half_field[:, :, 0]
    half_im = half_field[:, :, 1]
    if adjoint:
        half_re = half_re[..., :, None, :]
        half_im = half_im[..., :, None, :]
        out_re = lax.optimization_barrier(jnp.sum(link_re * half_re + link_im * half_im, axis=-3))
        out_im = lax.optimization_barrier(jnp.sum(link_re * half_im - link_im * half_re, axis=-3))
    else:
        half_re = half_re[..., None, :, :]
        half_im = half_im[..., None, :, :]
        out_re = lax.optimization_barrier(jnp.sum(link_re * half_re - link_im * half_im, axis=-2))
        out_im = lax.optimization_barrier(jnp.sum(link_re * half_im + link_im * half_re, axis=-2))
    return jnp.stack([out_re, out_im], axis=2).astype(jnp.bfloat16)

def apply_site(site_term, vectors):
    shape_in = vectors.shape
    spinor = vectors.astype(jnp.float32).reshape(shape_in[0], shape_in[1], 2, 2, 1, 6, shape_in[-1])
    matrix = site_term.astype(jnp.float32)[:, None]
    spin_re = spinor[:, :, 0]
    spin_im = spinor[:, :, 1]
    mat_re = matrix[:, :, :, 0]
    mat_im = matrix[:, :, :, 1]
    out_re = lax.optimization_barrier(jnp.sum(mat_re * spin_re - mat_im * spin_im, axis=-2))
    out_im = lax.optimization_barrier(jnp.sum(mat_re * spin_im + mat_im * spin_re, axis=-2))
    return jnp.stack([out_re, out_im], axis=2).reshape(shape_in).astype(jnp.bfloat16)

def contract(left, right):
    shape_two = (left.shape[0], left.shape[1], -1)
    left_re = left[:, :, 0].reshape(shape_two)
    left_im = left[:, :, 1].reshape(shape_two)
    right_re = right[:, :, 0].reshape(shape_two)
    right_im = right[:, :, 1].reshape(shape_two)
    first = jnp.concatenate([left_re, left_im], axis=-1).astype(jnp.float32)
    second = jnp.concatenate([right_re, right_im], axis=-1).astype(jnp.float32)
    third = jnp.concatenate([left_re, -left_im], axis=-1).astype(jnp.float32)
    fourth = jnp.concatenate([right_im, right_re], axis=-1).astype(jnp.float32)
    return (jnp.einsum('bik,bjk->bij', first, second), jnp.einsum('bik,bjk->bij', third, fourth))

def make_halves(vectors, links):
    result = []
    for direction in range(4):
        minus_half, plus_half = project(vectors, direction)
        back_half = transport(links[:, direction], plus_half, True)
        result.append((minus_half, plus_half, back_half))
    return result

def restrict(vectors, links, site_term, halves, incoming, select_sites):
    positions = jnp.arange(vectors.shape[-1], dtype=jnp.int32)
    self_re, self_im = contract(vectors, apply_site(site_term, vectors))
    blocks_out = []
    for direction in range(4):
        stride = site_strides[direction]
        coordinate = positions // stride % 4
        minus_half, plus_half, back_half = halves[direction]
        link_field = links[:, direction]
        keep_up = (coordinate < 3).astype(minus_half.dtype)
        keep_down = (coordinate > 0).astype(minus_half.dtype)
        ahead_field = transport(link_field, jnp.roll(minus_half, -stride, axis=-1) * keep_up, False)
        fwd_re, fwd_im = contract(minus_half, ahead_field)
        behind_field = jnp.roll(back_half, stride, axis=-1) * keep_down
        bwd_re, bwd_im = contract(plus_half, behind_field)
        self_re = self_re - 0.5 * (fwd_re + bwd_re)
        self_im = self_im - 0.5 * (fwd_im + bwd_im)
        from_above, from_below = incoming[direction]
        face_ahead = transport(select_sites(link_field, stride, 3), from_above, False)
        up_re, up_im = contract(select_sites(minus_half, stride, 3), face_ahead)
        down_re, down_im = contract(select_sites(plus_half, stride, 0), from_below)
        blocks_out.append(jnp.stack([up_re, up_im], 1) * (-0.5 * coarse_scale))
        blocks_out.append(jnp.stack([down_re, down_im], 1) * (-0.5 * coarse_scale))
    first_block = jnp.stack([self_re, self_im], 1) * coarse_scale
    return jnp.stack([first_block] + blocks_out, axis=1)

def complex_apply(coarse_f, stacked):
    mat_re = coarse_f[..., 0, :, :]
    mat_im = coarse_f[..., 1, :, :]
    vec_re = stacked[..., 0, :]
    vec_im = stacked[..., 1, :]
    highest = lax.Precision.HIGHEST
    out_re = jnp.einsum('...kij,...kj->...i', mat_re, vec_re, precision=highest) - jnp.einsum('...kij,...kj->...i', mat_im, vec_im, precision=highest)
    out_im = jnp.einsum('...kij,...kj->...i', mat_re, vec_im, precision=highest) + jnp.einsum('...kij,...kj->...i', mat_im, vec_re, precision=highest)
    return jnp.stack([out_re, out_im], axis=-2)

def inner_product(left, right):
    real_part = jnp.sum(left[..., 0, :] * right[..., 0, :] + left[..., 1, :] * right[..., 1, :])
    imag_part = jnp.sum(left[..., 0, :] * right[..., 1, :] - left[..., 1, :] * right[..., 0, :])
    return (real_part, imag_part)

def subtract_scaled(vector, coef, basis):
    new_re = vector[..., 0, :] - (coef[0] * basis[..., 0, :] - coef[1] * basis[..., 1, :])
    new_im = vector[..., 1, :] - (coef[0] * basis[..., 1, :] + coef[1] * basis[..., 0, :])
    return jnp.stack([new_re, new_im], axis=-2)

def complex_mul(first, second):
    return (first[0] * second[0] - first[1] * second[1], first[0] * second[1] + first[1] * second[0])

def rotate(top_entry, bottom_entry, scale_norm, upper_value, lower_value):
    conj_top = (top_entry[0], -top_entry[1])
    conj_bottom = (bottom_entry[0], -bottom_entry[1])
    part_one = complex_mul(conj_top, upper_value)
    part_two = complex_mul(conj_bottom, lower_value)
    part_three = complex_mul(bottom_entry, upper_value)
    part_four = complex_mul(top_entry, lower_value)
    new_upper = ((part_one[0] + part_two[0]) / scale_norm, (part_one[1] + part_two[1]) / scale_norm)
    new_lower = ((part_four[0] - part_three[0]) / scale_norm, (part_four[1] - part_three[1]) / scale_norm)
    return (new_upper, new_lower)

def least_squares(hessen, beta):
    columns = len(hessen[0])
    zero_value = jnp.zeros((), jnp.float32)
    matrix = [list(row_list) for row_list in hessen]
    target = [(beta, zero_value)] + [(zero_value, zero_value)] * columns
    rotations = []
    for col_index in range(columns):
        for rot_index in range(col_index):
            top_entry, bottom_entry, scale_norm = rotations[rot_index]
            pair = rotate(top_entry, bottom_entry, scale_norm, matrix[rot_index][col_index], matrix[rot_index + 1][col_index])
            matrix[rot_index][col_index] = pair[0]
            matrix[rot_index + 1][col_index] = pair[1]
        top_entry = matrix[col_index][col_index]
        bottom_entry = matrix[col_index + 1][col_index]
        scale_norm = jnp.sqrt(top_entry[0] * top_entry[0] + top_entry[1] * top_entry[1] + bottom_entry[0] * bottom_entry[0] + bottom_entry[1] * bottom_entry[1])
        rotations.append((top_entry, bottom_entry, scale_norm))
        matrix[col_index][col_index] = (scale_norm, zero_value)
        matrix[col_index + 1][col_index] = (zero_value, zero_value)
        pair = rotate(top_entry, bottom_entry, scale_norm, target[col_index], target[col_index + 1])
        target[col_index] = pair[0]
        target[col_index + 1] = pair[1]
    weights = [None] * columns
    for row_index in reversed(range(columns)):
        remainder = target[row_index]
        for col_index in range(row_index + 1, columns):
            product_term = complex_mul(matrix[row_index][col_index], weights[col_index])
            remainder = (remainder[0] - product_term[0], remainder[1] - product_term[1])
        weights[row_index] = (remainder[0] / matrix[row_index][row_index][0], remainder[1] / matrix[row_index][row_index][0])
    return weights

def rank_table(owner, owners_count):
    one_hot = (owner[..., None] == jnp.arange(owners_count, dtype=jnp.int32)).astype(jnp.int32)
    return lax.optimization_barrier(jnp.sum(jnp.cumsum(one_hot, axis=3) * one_hot, axis=-1)) - 1

def coarse_matvec(coarse_f, vector):
    neighbors = [vector]
    for axis_index in roll_axes:
        neighbors.append(jnp.roll(vector, -1, axis=axis_index))
        neighbors.append(jnp.roll(vector, 1, axis=axis_index))
    return complex_apply(coarse_f, jnp.stack(neighbors, axis=4))

def reference(vectors, links, site_term, owner, coarse_rhs):
    group_size = N_GX * AT
    block_count = N_GZ * N_GY
    flat_vec = vectors.reshape((block_count, group_size) + vectors.shape[4:])
    flat_link = links.reshape((block_count, group_size) + links.shape[4:])
    flat_site = site_term.reshape((block_count, group_size) + site_term.shape[4:])

    def send_faces(inputs):
        halves = make_halves(inputs[0], inputs[1])
        above_faces = []
        below_faces = []
        for direction in range(4):
            above_faces.append(take_sites(halves[direction][0], site_strides[direction], 0))
            below_faces.append(take_sites(halves[direction][2], site_strides[direction], 3))
        return tuple(above_faces) + tuple(below_faces)
    faces = lax.map(send_faces, (flat_vec, flat_link))
    moved = []
    for direction in range(4):
        grid_face = faces[direction].reshape((N_GZ, N_GY, N_GX, AT) + faces[direction].shape[2:])
        moved.append(jnp.roll(grid_face, -1, axis=roll_axes[direction]).reshape(faces[direction].shape))
    for direction in range(4):
        grid_face = faces[4 + direction].reshape((N_GZ, N_GY, N_GX, AT) + faces[4 + direction].shape[2:])
        moved.append(jnp.roll(grid_face, 1, axis=roll_axes[direction]).reshape(faces[4 + direction].shape))

    def coarse_block(inputs):
        halves = make_halves(inputs[0], inputs[1])
        incoming = []
        for direction in range(4):
            incoming.append((inputs[3 + direction], inputs[7 + direction]))
        return restrict(inputs[0], inputs[1], inputs[2], halves, incoming, take_sites)
    blocks = lax.map(coarse_block, (flat_vec, flat_link, flat_site) + tuple(moved))
    coarse_rows = blocks.reshape((N_GZ, N_GY, N_GX, AT, 9, 2, NV, NV)).astype(jnp.bfloat16)
    coarse_f = coarse_rows.astype(jnp.float32)
    right_side = coarse_rhs.astype(jnp.float32)
    zero_value = jnp.zeros((), jnp.float32)
    beta = jnp.sqrt(jnp.sum(right_side * right_side) + epsilon)
    basis = [right_side / beta]
    hessen = []
    for row_index in range(ITERS + 1):
        hessen.append([(zero_value, zero_value)] * ITERS)
    for column in range(ITERS):
        work = coarse_matvec(coarse_f, basis[column])
        for row_index in range(column + 1):
            coef = inner_product(basis[row_index], work)
            hessen[row_index][column] = coef
            work = subtract_scaled(work, coef, basis[row_index])
        norm_now = jnp.sqrt(jnp.sum(work * work) + epsilon)
        hessen[column + 1][column] = (norm_now, zero_value)
        basis.append(work / norm_now)
    weights = least_squares(hessen, beta)
    solution = jnp.zeros_like(right_side)
    for column in range(ITERS):
        solution = subtract_scaled(solution, (-weights[column][0], -weights[column][1]), basis[column])
    owners_count = N_GZ * N_GX
    owner_rank = rank_table(owner, owners_count)
    coord_z = lax.broadcasted_iota(jnp.int32, owner.shape, 0)
    coord_y = lax.broadcasted_iota(jnp.int32, owner.shape, 1)
    coord_x = lax.broadcasted_iota(jnp.int32, owner.shape, 2)
    location = (owner * CAP + ((coord_z * N_GX + coord_x) * N_GY + coord_y) * PAIR + owner_rank).reshape(-1).astype(jnp.int32)
    rows_out = jnp.zeros((owners_count * CAP, 9, 2, NV * NV), jnp.bfloat16)
    rows_out = rows_out.at[location].set(coarse_rows.reshape(-1, 9, 2, NV * NV))
    solution_out = jnp.zeros((owners_count * CAP, 2, NV), jnp.float32)
    solution_out = solution_out.at[location].set(solution.reshape(-1, 2, NV))
    return (rows_out.reshape(owners_count, CAP, 9, 2, NV * NV), solution_out.reshape(owners_count, CAP, 2, NV))
```

```python
import jax
import jax.numpy as jnp
import numpy as np
from jax import lax
from jax.experimental import pallas as pl
from jax.experimental.pallas import tpu as pltpu
from jax.sharding import PartitionSpec as P

NV = 24
AT = 4
ITERS = 4
PAIR = 1
LANES = 128
GROUP = LANES // NV
CHUNKS = -(-NV // GROUP)
ROWS = 2 * AT
TILES = 9 * CHUNKS
WIDE = (TILES + 1) * LANES
MESH = pl.DeviceIdType.MESH


coarse_scale = 1.0 / 256.0
epsilon = 1e-06
site_strides = (64, 16, 4, 1)
neighbor_offsets = (
    (0, 0, 0, 0),
    (0, 0, 1, 0),
    (0, 0, -1, 0),
    (0, 1, 0, 0),
    (0, -1, 0, 0),
    (1, 0, 0, 0),
    (-1, 0, 0, 0),
    (0, 0, 0, 1),
    (0, 0, 0, -1),
)


lower_table = (
    (((1, 3, 1), (0, 3, -1)), ((1, 2, 1), (0, 2, -1))),
    (((0, 3, -1), (1, 3, -1)), ((0, 2, 1), (1, 2, 1))),
    (((1, 2, 1), (0, 2, -1)), ((1, 3, -1), (0, 3, 1))),
    (((0, 2, 1), (1, 2, 1)), ((0, 3, 1), (1, 3, 1))),
)


def from_behind(block, axis, distance):
    devices = range(lax.axis_size(axis))
    route = [((i - distance) % len(devices), i) for i in devices]
    return lax.ppermute(block, axis, route)


def rounded(value):
    return value.astype(jnp.bfloat16).astype(jnp.float32)


def half(vec_ref, direction, spin, colour, sign):
    pair = []
    for part in range(2):
        from_part, from_spin, factor = lower_table[direction][spin][part]
        upper = vec_ref[0, part * 12 + spin * 3 + colour].astype(jnp.float32)
        lower = vec_ref[0, from_part * 12 + from_spin * 3 + colour].astype(jnp.float32)
        pair.append(rounded(upper + (sign * factor) * lower))
    return pair


def link(link_ref, direction, part, row, col):
    at = direction * 18 + part * 9 + row * 3 + col
    return link_ref[0, at : at + 1, :]


def halves_kernel(vec_ref, link_ref, minus_ref, back_ref):
    for mu in range(4):
        for spin in range(2):
            plus = []
            for col in range(3):
                minus = half(vec_ref, mu, spin, col, -1)
                plus.append(half(vec_ref, mu, spin, col, 1))
                for part in range(2):
                    minus_ref[mu, 0, part * 6 + spin * 3 + col] = minus[part].astype(jnp.bfloat16)
            for col in range(3):
                out_re, out_im = 0.0, 0.0
                for row in range(3):
                    u_re = link(link_ref, mu, 0, row, col)
                    u_im = link(link_ref, mu, 1, row, col)
                    p_re, p_im = plus[row]
                    out_re = out_re + u_re * p_re + u_im * p_im
                    out_im = out_im + u_re * p_im - u_im * p_re
                back_ref[mu, 0, spin * 3 + col] = out_re.astype(jnp.bfloat16)
                back_ref[mu, 0, 6 + spin * 3 + col] = out_im.astype(jnp.bfloat16)


def contract(left, right):
    return lax.dot_general(
        jnp.concatenate(left, axis=1),
        jnp.concatenate(right, axis=1),
        (((1,), (1,)), ((), ())),
        preferred_element_type=jnp.float32,
    )


def stacked(pieces):
    return jnp.concatenate(pieces, axis=0).astype(jnp.bfloat16)


def merged(product):
    lane = lax.broadcasted_iota(jnp.int32, (NV, LANES), 1)
    wide = jnp.concatenate([product, jnp.zeros((2 * NV, LANES - 4 * NV), jnp.float32)], axis=1)
    low = wide[NV:]
    crossed = jnp.where(
        lane // NV % 2 == 0, pltpu.roll(low, LANES - NV, 1), -pltpu.roll(low, NV, 1)
    )
    return wide[:NV] + crossed


def restrict_kernel(vec_ref, link_ref, site_ref, rhs_ref, minus_ref, back_ref, *rest):
    near_minus, near_back = rest[0:4], rest[4:8]
    msg_ref, block_ref, flat_ref = rest[8:]
    step = pl.program_id(0)
    sites = vec_ref.shape[-1]
    lane8 = lax.broadcasted_iota(jnp.int32, (8, LANES), 1)
    block_ref[NV:] = jnp.zeros((block_ref.shape[0] - NV, LANES), jnp.float32)

    def emit(k, block):
        block_ref[:NV] = rounded(block)
        pieces = [jnp.zeros((8, LANES), jnp.float32)] * 2
        for at in range(GROUP):
            rows = block_ref[pl.ds(at, 8, stride=GROUP), :]
            for part in range(2):
                shift = (at - part) * NV % LANES
                moved = rows if shift == 0 else pltpu.roll(rows, shift, 1)
                pieces[part] = jnp.where(lane8 // NV == at, moved, pieces[part])
        for part in range(2):
            flat_ref[k, pl.ds(pl.multiple_of(step * 16 + part * 8, 8), 8), :] = pieces[part]

    left, right = [], []
    for chirality in range(2):
        for i in range(6):
            out_re, out_im = 0.0, 0.0
            for j in range(6):
                at = chirality * 72 + i * 6 + j
                m_re = site_ref[0, at : at + 1, :]
                m_im = site_ref[0, at + 36 : at + 37, :]
                v_re = vec_ref[0, chirality * 6 + j].astype(jnp.float32)
                v_im = vec_ref[0, 12 + chirality * 6 + j].astype(jnp.float32)
                out_re = out_re + m_re * v_re - m_im * v_im
                out_im = out_im + m_re * v_im + m_im * v_re
            right.append(stacked([out_re, out_im, out_re, out_im]))
            at = chirality * 6 + i
            left.append(
                stacked([vec_ref[0, at].astype(jnp.float32), vec_ref[0, 12 + at].astype(jnp.float32)])
            )
    own = merged(contract(left, right))
    position = lax.broadcasted_iota(jnp.int32, (NV, sites), 1)
    for mu in range(4):
        stride = site_strides[mu]
        coordinate = position // stride % 4
        last = coordinate == 3
        first = coordinate == 0

        def split(pair, edge):
            return stacked(
                [jnp.where(edge, 0.0, part) for part in pair]
                + [jnp.where(edge, part, 0.0) for part in pair]
            )

        def shifted(own, near, edge, own_shift, near_shift):
            return jnp.where(
                edge,
                pltpu.roll(near.astype(jnp.float32), near_shift, 1),
                pltpu.roll(own.astype(jnp.float32), own_shift, 1),
            )

        left, right = [], []
        for spin in range(2):
            field = []
            for col in range(3):
                at = spin * 3 + col
                field.append(
                    [
                        shifted(
                            minus_ref[mu, 0, part * 6 + at],
                            near_minus[mu][0, part * 6 + at],
                            last,
                            sites - stride,
                            3 * stride,
                        )
                        for part in range(2)
                    ]
                )
            for row in range(3):
                out_re, out_im = 0.0, 0.0
                for col in range(3):
                    u_re = link(link_ref, mu, 0, row, col)
                    u_im = link(link_ref, mu, 1, row, col)
                    f_re, f_im = field[col]
                    out_re = out_re + u_re * f_re - u_im * f_im
                    out_im = out_im + u_re * f_im + u_im * f_re
                right.append(split((out_re, out_im), last))
                at = spin * 3 + row
                left.append(
                    stacked([minus_ref[mu, 0, part * 6 + at].astype(jnp.float32) for part in range(2)])
                )
        both = merged(contract(left, right))
        own = own - 0.5 * both
        emit(2 * mu + 1, pltpu.roll(both, LANES - 2 * NV, 1) * (-0.5 * coarse_scale))
        left, right = [], []
        for spin in range(2):
            for col in range(3):
                at = spin * 3 + col
                pair = [
                    shifted(
                        back_ref[mu, 0, part * 6 + at],
                        near_back[mu][0, part * 6 + at],
                        first,
                        stride,
                        sites - 3 * stride,
                    )
                    for part in range(2)
                ]
                right.append(split(pair, first))
                left.append(stacked(half(vec_ref, mu, spin, col, 1)))
        both = merged(contract(left, right))
        own = own - 0.5 * both
        emit(2 * mu + 2, pltpu.roll(both, LANES - 2 * NV, 1) * (-0.5 * coarse_scale))
    emit(0, own * coarse_scale)

    @pl.when(step == AT - 1)
    def _():
        for k in range(9):
            for chunk in range(CHUNKS):
                at = (k * CHUNKS + chunk) * LANES
                msg_ref[:, at : at + LANES] = flat_ref[
                    k, pl.ds(chunk, ROWS, stride=8), :
                ].astype(jnp.bfloat16)
        msg_ref[:, TILES * LANES :] = rhs_ref[...]


def fine_message(vectors, links, site_term, rhs):
    sites = vectors.shape[-1]
    vec = jnp.transpose(vectors, (0, 2, 3, 4, 1, 5)).reshape(AT, 24, NV, sites)
    link_f = links.astype(jnp.float32).reshape(AT, 72, sites)
    site_f = site_term.astype(jnp.float32).reshape(AT, 144, sites)
    tiled = jnp.concatenate(
        [rhs.reshape(ROWS, NV)] * GROUP + [jnp.zeros((ROWS, LANES - GROUP * NV), rhs.dtype)], axis=1
    )
    vec_spec = pl.BlockSpec((1, 24, NV, sites), lambda a: (a, 0, 0, 0))
    link_spec = pl.BlockSpec((1, 72, sites), lambda a: (a, 0, 0))
    site_spec = pl.BlockSpec((1, 144, sites), lambda a: (a, 0, 0))
    rhs_spec = pl.BlockSpec((ROWS, LANES), lambda a: (0, 0))
    half_spec = pl.BlockSpec((4, 1, 12, NV, sites), lambda a: (0, a, 0, 0, 0))
    near_spec = pl.BlockSpec((1, 12, NV, sites), lambda a: (a, 0, 0, 0))
    half_shape = jax.ShapeDtypeStruct((4, AT, 12, NV, sites), jnp.bfloat16)
    params = pltpu.CompilerParams(vmem_limit_bytes=48 << 20)
    minus, back = pl.pallas_call(
        halves_kernel,
        grid=(AT,),
        in_specs=[vec_spec, link_spec],
        out_specs=[half_spec, half_spec],
        out_shape=(half_shape, half_shape),
        compiler_params=params,
    )(vec, link_f)
    axes = ("gx", "gy", "gz")
    near_minus = [from_behind(minus[mu], axes[mu], -1) for mu in range(3)]
    near_back = [from_behind(back[mu], axes[mu], 1) for mu in range(3)]
    near_minus.append(jnp.roll(minus[3], -1, axis=0))
    near_back.append(jnp.roll(back[3], 1, axis=0))
    return pl.pallas_call(
        restrict_kernel,
        grid=(AT,),
        in_specs=[vec_spec, link_spec, site_spec, rhs_spec, half_spec, half_spec] + [near_spec] * 8,
        out_specs=pl.BlockSpec((ROWS, WIDE), lambda a: (0, 0)),
        out_shape=jax.ShapeDtypeStruct((ROWS, WIDE), jnp.bfloat16),
        scratch_shapes=[
            pltpu.VMEM((8 * GROUP, LANES), jnp.float32),
            pltpu.VMEM((9, 8 * ROWS, LANES), jnp.float32),
        ],
        compiler_params=params,
    )(vec, link_f, site_f, tiled, minus, back, *near_minus, *near_back)


def complex_mul(first, second):
    return (
        first[0] * second[0] - first[1] * second[1],
        first[0] * second[1] + first[1] * second[0],
    )


def rotate(top_entry, bottom_entry, scale_norm, upper_value, lower_value):
    conj_top = (top_entry[0], -top_entry[1])
    conj_bottom = (bottom_entry[0], -bottom_entry[1])
    part_one = complex_mul(conj_top, upper_value)
    part_two = complex_mul(conj_bottom, lower_value)
    part_three = complex_mul(bottom_entry, upper_value)
    part_four = complex_mul(top_entry, lower_value)
    new_upper = ((part_one[0] + part_two[0]) / scale_norm, (part_one[1] + part_two[1]) / scale_norm)
    new_lower = (
        (part_four[0] - part_three[0]) / scale_norm,
        (part_four[1] - part_three[1]) / scale_norm,
    )
    return (new_upper, new_lower)


def least_squares(hessen, beta):
    columns = len(hessen[0])
    zero_value = jnp.zeros((), jnp.float32)
    matrix = [list(row_list) for row_list in hessen]
    target = [(beta, zero_value)] + [(zero_value, zero_value)] * columns
    rotations = []
    for col_index in range(columns):
        for rot_index in range(col_index):
            top_entry, bottom_entry, scale_norm = rotations[rot_index]
            pair = rotate(
                top_entry,
                bottom_entry,
                scale_norm,
                matrix[rot_index][col_index],
                matrix[rot_index + 1][col_index],
            )
            matrix[rot_index][col_index] = pair[0]
            matrix[rot_index + 1][col_index] = pair[1]
        top_entry = matrix[col_index][col_index]
        bottom_entry = matrix[col_index + 1][col_index]
        scale_norm = jnp.sqrt(
            top_entry[0] * top_entry[0]
            + top_entry[1] * top_entry[1]
            + bottom_entry[0] * bottom_entry[0]
            + bottom_entry[1] * bottom_entry[1]
        )
        rotations.append((top_entry, bottom_entry, scale_norm))
        matrix[col_index][col_index] = (scale_norm, zero_value)
        matrix[col_index + 1][col_index] = (zero_value, zero_value)
        pair = rotate(top_entry, bottom_entry, scale_norm, target[col_index], target[col_index + 1])
        target[col_index] = pair[0]
        target[col_index + 1] = pair[1]
    weights = [None] * columns
    for row_index in reversed(range(columns)):
        remainder = target[row_index]
        for col_index in range(row_index + 1, columns):
            product_term = complex_mul(matrix[row_index][col_index], weights[col_index])
            remainder = (remainder[0] - product_term[0], remainder[1] - product_term[1])
        weights[row_index] = (
            remainder[0] / matrix[row_index][row_index][0],
            remainder[1] / matrix[row_index][row_index][0],
        )
    return weights


def split_two(value):
    high = value.astype(jnp.bfloat16)
    low = (value - high.astype(jnp.float32)).astype(jnp.bfloat16)
    return high, low


def gather_kernel(msg_ref, out_ref, chain_sem, plane_sem, cross_sem, core_sem, recv_sem, own_sem):
    size_z, size_y, size_x = (lax.axis_size(name) for name in ("gz", "gy", "gx"))
    z, y, x = (lax.axis_index(name) for name in ("gz", "gy", "gx"))
    middle = TILES // 2 * LANES
    spans = (pl.ds(0, middle), pl.ds(middle, WIDE - middle))

    def flipped(bits):
        low, high = z % 2, z // 2
        if bits & 1:
            low = 1 - low
        if bits & 2:
            high = 1 - high
        return high * 2 + low

    def slot(at_z, at_y, at_x):
        return (at_z * size_y + at_y) * size_x + at_x

    def copy(source, at, part, sem, target):
        return pltpu.make_async_remote_copy(
            src_ref=source.at[:, spans[part]],
            dst_ref=out_ref.at[at, :, spans[part]],
            send_sem=sem,
            recv_sem=recv_sem.at[at, part],
            device_id=target,
            device_id_type=MESH,
        )

    others = [(y + step) % size_y for step in range(1, size_y)]
    sides = ((x > 0, x - 1), (x < size_x - 1, x + 1))
    barrier = pltpu.get_barrier_semaphore()
    for bits in (1, 2):
        pl.semaphore_signal(
            barrier, inc=1, device_id=(flipped(bits), y, x), device_id_type=MESH
        )
    for other in others:
        pl.semaphore_signal(barrier, inc=1, device_id=(z, other, x), device_id_type=MESH)
    for exists, at in sides:

        @pl.when(exists)
        def _():
            pl.semaphore_signal(barrier, inc=1, device_id=(z, y, at), device_id_type=MESH)

    inner = (x > 0).astype(jnp.int32) + (x < size_x - 1).astype(jnp.int32)
    pl.semaphore_wait(barrier, 1 + size_y + inner)

    mine = slot(z, y, x)
    keep = pltpu.make_async_copy(msg_ref, out_ref.at[mine], own_sem)
    keep.start()

    def to_side(source, at_x, side, part):
        return copy(
            source, slot(z, y, at_x), part, chain_sem.at[side, at_x, part], (z, y, sides[side][1])
        )

    def to_plane(source, at_x, which, part):
        return copy(
            source,
            slot(z, y, at_x),
            part,
            plane_sem.at[which, at_x, part],
            (flipped(which + 1), y, x),
        )

    def to_cross(at_x, which):
        at = slot(flipped(which + 1), y, at_x)
        return copy(
            out_ref.at[at], at, which, cross_sem.at[which, at_x], (flipped(2 - which), y, x)
        )

    def to_core(source, bits, at_x, which, part):
        at = slot(flipped(bits), y, at_x)
        return copy(source, at, part, core_sem.at[which, bits, at_x, part], (z, others[which], x))

    def arrived(at, part):
        copy(out_ref.at[at], at, part, own_sem, (z, others[0], x)).wait_recv()

    def spread(source, at_x, toward):
        for part in range(2):
            for side in toward:

                @pl.when(sides[side][0])
                def _():
                    to_side(source, at_x, side, part).start()

            for which in range(2):
                to_plane(source, at_x, which, part).start()
            for which in range(len(others)):
                to_core(source, 0, at_x, which, part).start()

    def column(at_x, toward):
        at = slot(z, y, at_x)
        for part in range(2):
            arrived(at, part)
        spread(out_ref.at[at], at_x, toward)

    def next_plane(at_x):
        for which in range(2):
            at = slot(flipped(which + 1), y, at_x)
            for part in (which, 1 - which):
                arrived(at, part)
                if part == which:
                    to_cross(at_x, which).start()
                for other in range(len(others)):
                    to_core(out_ref.at[at], which + 1, at_x, other, part).start()

    def far_plane(at_x):
        at = slot(flipped(3), y, at_x)
        for part in range(2):
            arrived(at, part)
            for other in range(len(others)):
                to_core(out_ref.at[at], 3, at_x, other, part).start()

    def at_distance(distance, action):
        if distance == 0:
            action(x, None)
            return

        @pl.when(x >= distance)
        def _():
            action(x - distance, 1)

        @pl.when(x + distance < size_x)
        def _():
            action(x + distance, 0)

    spread(msg_ref, x, (0, 1))
    for distance in range(1, size_x + 2):
        if distance < size_x:
            at_distance(distance, lambda at_x, side: column(at_x, (side,)))
        if distance - 1 < size_x:
            at_distance(distance - 1, lambda at_x, side: next_plane(at_x))
        if 0 <= distance - 2 < size_x:
            at_distance(distance - 2, lambda at_x, side: far_plane(at_x))
    keep.wait()
    for at_x in range(size_x):
        for bits in range(4):
            for other in others:
                for part in range(2):
                    arrived(slot(flipped(bits), other, at_x), part)
    for at_x in range(size_x):
        for part in range(2):

            @pl.when((x > 0) & (x <= at_x))
            def _():
                to_side(msg_ref, at_x, 0, part).wait_send()

            @pl.when((x < size_x - 1) & (x >= at_x))
            def _():
                to_side(msg_ref, at_x, 1, part).wait_send()

            for which in range(2):
                to_plane(msg_ref, at_x, which, part).wait_send()
            for bits in range(4):
                for which in range(len(others)):
                    to_core(msg_ref, bits, at_x, which, part).wait_send()
        for which in range(2):
            to_cross(at_x, which).wait_send()


def gather_messages(message):
    size_z, size_y, size_x = (lax.axis_size(name) for name in ("gz", "gy", "gx"))
    assert size_z == 4
    devices = size_z * size_y * size_x
    dma = pltpu.SemaphoreType.DMA
    return pl.pallas_call(
        gather_kernel,
        out_shape=jax.ShapeDtypeStruct((devices, ROWS, WIDE), jnp.bfloat16),
        in_specs=[pl.BlockSpec(memory_space=pltpu.VMEM)],
        out_specs=pl.BlockSpec(memory_space=pltpu.VMEM),
        scratch_shapes=[
            dma((2, size_x, 2)),
            dma((2, size_x, 2)),
            dma((2, size_x)),
            dma((size_y - 1, 4, size_x, 2)),
            dma((devices, 2)),
            dma,
        ],
        compiler_params=pltpu.CompilerParams(
            collective_id=1, has_side_effects=True, vmem_limit_bytes=48 << 20
        ),
    )(message)


def total(value):
    return jnp.sum(jnp.sum(value, axis=0, keepdims=True), axis=1, keepdims=True)


def paired(value):
    row = lax.broadcasted_iota(jnp.int32, value.shape, 0)
    count = value.shape[0]
    return jnp.where(row % 2 == 0, pltpu.roll(value, count - 1, 0), pltpu.roll(value, 1, 0))


def gmres_kernel(sizes, pick_ref, rows_ref, reduce_ref, op_ref, sol_ref, acc_ref, one_ref, two_ref):
    size_z, size_y, size_x = sizes
    devices = size_z * size_y * size_x
    count = devices * ROWS
    row = lax.broadcasted_iota(jnp.int32, (count, LANES), 0)
    lane = lax.broadcasted_iota(jnp.int32, (count, LANES), 1)
    sign = jnp.where(row % 2 == 0, 1.0, -1.0)
    even8 = lax.broadcasted_iota(jnp.int32, (ROWS, LANES), 0) % 2 == 0
    lane8 = lax.broadcasted_iota(jnp.int32, (ROWS, LANES), 1)
    real = lane < NV

    def tile(ref, at):
        return ref[pl.ds(pl.multiple_of(at * ROWS, ROWS), ROWS), :]

    def apply(vector, swapped):
        one_ref[...] = vector * sign
        two_ref[...] = swapped

        @pl.loop(0, devices)
        def _(at):
            x = at % size_x
            y = at // size_x % size_y
            z = at // (size_x * size_y)

            def slot(at_z, at_y, at_x):
                return (at_z * size_y + at_y) * size_x + at_x

            places = (
                slot(z, y, (x + 1) % size_x),
                slot(z, y, (x + size_x - 1) % size_x),
                slot(z, (y + 1) % size_y, x),
                slot(z, (y + size_y - 1) % size_y, x),
                slot((z + 1) % size_z, y, x),
                slot((z + size_z - 1) % size_z, y, x),
            )
            near = []
            for ref in (one_ref, two_ref):
                own = tile(ref, at)
                near.append(
                    [own]
                    + [tile(ref, place) for place in places]
                    + [pltpu.roll(own, ROWS - 2, 0), pltpu.roll(own, 2, 0)]
                )
            for chunk in range(CHUNKS):
                sums = [0.0, 0.0]
                for k in range(9):
                    start = (k * CHUNKS + chunk) * LANES
                    rows = rows_ref[at, :, start : start + LANES].astype(jnp.float32)
                    for part in range(2):
                        sums[part] = sums[part] + rows * near[part][k]
                acc_ref[
                    pl.ds(pl.multiple_of(at * ROWS, ROWS), ROWS), chunk * LANES : (chunk + 1) * LANES
                ] = jnp.where(
                    even8,
                    sums[0] + pltpu.roll(sums[0], ROWS - 1, 0),
                    sums[1] + pltpu.roll(sums[1], 1, 0),
                )

        high, low = split_two(acc_ref[...])
        return jnp.dot(high, reduce_ref[...], preferred_element_type=jnp.float32) + jnp.dot(
            low, reduce_ref[...], preferred_element_type=jnp.float32
        )

    for z in range(size_z):
        for y in range(size_y):
            for x in range(size_x):
                at = (z * size_y + y) * size_x + x
                place = (z * size_x + x) * size_y + y
                chosen = pick_ref[at]

                @pl.when(chosen < 0)
                def _():
                    op_ref[place] = jnp.zeros(op_ref.shape[1:], op_ref.dtype)

                @pl.when(chosen >= 0)
                def _():
                    shift = (ROWS - 2 * chosen) % ROWS
                    for k in range(9):
                        turned = []
                        for chunk in range(CHUNKS):
                            start = (k * CHUNKS + chunk) * LANES
                            rows = rows_ref[at, :, start : start + LANES].astype(jnp.float32)
                            rows = pltpu.roll(rows, shift, 0)
                            back = chunk * (LANES - GROUP * NV)
                            turned.append(rows if back == 0 else pltpu.roll(rows, LANES - back, 1))
                        for chunk in range(CHUNKS):
                            start = chunk * LANES
                            width = min(LANES, NV * NV - start)
                            value = turned[chunk]
                            if chunk + 1 < CHUNKS:
                                cut = GROUP * NV - chunk * (LANES - GROUP * NV)
                                value = jnp.where(lane8 < cut, value, turned[chunk + 1])
                            op_ref[place, k, :, start : start + width] = value[:2, :width].astype(
                                jnp.bfloat16
                            )

    right_side = rows_ref[:, :, TILES * LANES :].astype(jnp.float32).reshape(count, LANES)
    zero_value = jnp.zeros((1, 1), jnp.float32)

    def squares(value):
        return total(jnp.where(real, value * value, 0.0))

    beta = jnp.sqrt(squares(right_side) + epsilon)
    basis = [right_side / beta]
    swapped = [paired(basis[0])]
    hessen = []
    for row_index in range(ITERS + 1):
        hessen.append([(zero_value, zero_value)] * ITERS)
    for column in range(ITERS):
        work = apply(basis[column], swapped[column])
        for row_index in range(column + 1):
            turned = swapped[row_index] * sign
            coef_re = total(jnp.where(real, basis[row_index] * work, 0.0))
            coef_im = -total(jnp.where(real, turned * work, 0.0))
            hessen[row_index][column] = (coef_re, coef_im)
            work = work - coef_re * basis[row_index] + coef_im * turned
        norm_now = jnp.sqrt(squares(work) + epsilon)
        hessen[column + 1][column] = (norm_now, zero_value)
        if column + 1 < ITERS:
            basis.append(work / norm_now)
            swapped.append(paired(basis[-1]))
    weights = least_squares(hessen, beta)
    answer = jnp.zeros_like(right_side)
    for column in range(ITERS):
        answer = (
            answer
            + weights[column][0] * basis[column]
            - weights[column][1] * (swapped[column] * sign)
        )
    one_ref[...] = answer
    for z in range(size_z):
        for y in range(size_y):
            for x in range(size_x):
                at = (z * size_y + y) * size_x + x
                chosen = pick_ref[at]
                shift = (ROWS - 2 * jnp.maximum(chosen, 0)) % ROWS
                rows = pltpu.roll(one_ref[at * ROWS : (at + 1) * ROWS], shift, 0)
                rows = jnp.where(chosen >= 0, rows, 0.0)
                sol_ref[(z * size_x + x) * size_y + y] = rows[:2, :NV]


def reduce_table():
    table = np.zeros((CHUNKS, LANES, LANES), np.float32)
    for chunk in range(CHUNKS):
        for at in range(GROUP):
            out = chunk * GROUP + at
            if out < NV:
                for copy in range(GROUP):
                    table[chunk, at * NV : (at + 1) * NV, copy * NV + out] = 1.0
    return table.reshape(CHUNKS * LANES, LANES).astype(jnp.bfloat16)


def coarse_solve(rows, owner):
    sizes = tuple(lax.axis_size(name) for name in ("gz", "gy", "gx"))
    devices, count = rows.shape[0], rows.shape[0] * ROWS
    mine = owner.reshape(-1, AT) == lax.axis_index(("gz", "gx"))
    chosen = jnp.max(jnp.where(mine, jnp.arange(AT, dtype=jnp.int32), -1), axis=1)
    vmem = pl.BlockSpec(memory_space=pltpu.VMEM)
    return pl.pallas_call(
        lambda *refs: gmres_kernel(sizes, *refs),
        out_shape=(
            jax.ShapeDtypeStruct((devices, 9, 2, NV * NV), jnp.bfloat16),
            jax.ShapeDtypeStruct((devices, 2, NV), jnp.float32),
        ),
        in_specs=[pl.BlockSpec(memory_space=pltpu.SMEM), vmem, vmem],
        out_specs=[vmem, vmem],
        scratch_shapes=[
            pltpu.VMEM((count, CHUNKS * LANES), jnp.float32),
            pltpu.VMEM((count, LANES), jnp.float32),
            pltpu.VMEM((count, LANES), jnp.float32),
        ],
        compiler_params=pltpu.CompilerParams(vmem_limit_bytes=60 << 20),
    )(chosen, rows, reduce_table())


def on_device(vectors, links, site_term, owner, coarse_rhs):
    message = fine_message(
        vectors[0, 0, 0], links[0, 0, 0], site_term[0, 0, 0], coarse_rhs[0, 0, 0]
    )
    rows = gather_messages(message)
    operator, answer = coarse_solve(rows, owner)
    return operator[None], answer[None]


def solution(mesh):
    return jax.shard_map(
        on_device,
        mesh=mesh,
        in_specs=(
            P("gz", "gy", "gx", None, None, None, None, None, None),
            P("gz", "gy", "gx", None, None, None, None, None, None),
            P("gz", "gy", "gx", None, None, None, None, None, None),
            P(),
            P("gz", "gy", "gx", None, None, None),
        ),
        out_specs=(P(("gz", "gx"), None, None, None, None), P(("gz", "gx"), None, None, None)),
        check_vma=False,
    )
```

```python
import jax
import jax.numpy as jnp
import numpy as np
from jax import lax
from jax.experimental import pallas as pl
from jax.experimental.pallas import tpu as pltpu
from jax.sharding import PartitionSpec as P

NV = 24
AT = 4
ITERS = 4
PAIR = 1
LANES = 128
GROUP = LANES // NV
CHUNKS = -(-NV // GROUP)
ROWS = 2 * AT
TILES = 9 * CHUNKS
WIDE = (TILES + 1) * LANES
MESH = pl.DeviceIdType.MESH


coarse_scale = 1.0 / 256.0
epsilon = 1e-06
site_strides = (64, 16, 4, 1)
lower_table = (
    (((1, 3, 1), (0, 3, -1)), ((1, 2, 1), (0, 2, -1))),
    (((0, 3, -1), (1, 3, -1)), ((0, 2, 1), (1, 2, 1))),
    (((1, 2, 1), (0, 2, -1)), ((1, 3, -1), (0, 3, 1))),
    (((0, 2, 1), (1, 2, 1)), ((0, 3, 1), (1, 3, 1))),
)


def rounded(value):
    return value.astype(jnp.bfloat16).astype(jnp.float32)


def face_table():
    table = np.zeros((4, 2, 2, 256, 2, 64), np.float32)
    place = np.arange(64)
    for mu, stride in enumerate(site_strides):
        for layer in range(2):
            site = place // stride * 4 * stride + place % stride + 3 * layer * stride
            for spin in range(2):
                table[mu, layer, spin, site, spin, place] = 1.0
    return table.reshape(4, 2, 512, LANES).astype(jnp.bfloat16)


def halved(field, direction, spin, sign):
    pair = []
    for part in range(2):
        from_part, from_spin, factor = lower_table[direction][spin][part]
        lower = field[from_part][from_spin]
        upper = field[part][spin]
        pair.append(upper + lower if sign * factor > 0 else upper - lower)
    return pair


def link(link_ref, at, direction, part, row, col):
    index = direction * 18 + part * 9 + row * 3 + col
    return link_ref[at, index : index + 1, :]


def stacked(pieces):
    return jnp.concatenate(pieces, axis=0).astype(jnp.bfloat16)


def across(left, right):
    return lax.dot_general(
        left, right, (((1,), (1,)), ((), ())), preferred_element_type=jnp.float32
    )


def packed(operand, table):
    rows = jnp.concatenate([operand[:, at * 512 : (at + 1) * 512] for at in range(3)], axis=0)
    out = jnp.dot(rows, table, preferred_element_type=jnp.float32)
    return [out[at * 2 * NV : (at + 1) * 2 * NV] for at in range(3)]


def store_face(ref, index, pieces):
    for at, piece in enumerate(pieces):
        ref[index + (slice(None), slice(at * LANES, (at + 1) * LANES))] = piece.astype(jnp.bfloat16)


def faces_kernel(vec_ref, link_ref, table_ref, face_ref):
    field = [
        [
            [vec_ref[0, part * 12 + spin * 3 + col].astype(jnp.float32) for spin in range(4)]
            for part in range(2)
        ]
        for col in range(3)
    ]
    for mu in range(3):
        sides = []
        for sign in (-1, 1):
            pieces = []
            for col in range(3):
                for spin in range(2):
                    pieces.append(stacked(halved(field[col], mu, spin, sign)))
            sides.append(jnp.concatenate(pieces, axis=1))
        store_face(face_ref, (2 * mu, 0), packed(sides[0], table_ref[mu, 0]))
        plus = packed(sides[1], table_ref[mu, 1])
        rows = link_ref[0, mu * 18 : (mu + 1) * 18, :].astype(jnp.bfloat16)
        links = jnp.dot(
            rows, table_ref[mu, 1, :256], preferred_element_type=jnp.float32
        ) + jnp.dot(rows, table_ref[mu, 1, 256:], preferred_element_type=jnp.float32)
        back = []
        for col in range(3):
            out_re, out_im = 0.0, 0.0
            for row in range(3):
                at = row * 3 + col
                u_re, u_im = links[at : at + 1], links[9 + at : 10 + at]
                p_re, p_im = plus[row][:NV], plus[row][NV:]
                out_re = out_re + u_re * p_re + u_im * p_im
                out_im = out_im + u_re * p_im - u_im * p_re
            back.append(jnp.concatenate([out_re, out_im], axis=0))
        store_face(face_ref, (2 * mu + 1, 0), back)


def merged(product):
    lane = lax.broadcasted_iota(jnp.int32, (NV, LANES), 1)
    wide = jnp.concatenate([product, jnp.zeros((2 * NV, LANES - 2 * NV), jnp.float32)], axis=1)
    low = wide[NV:]
    crossed = jnp.where(lane < NV, pltpu.roll(low, LANES - NV, 1), -pltpu.roll(low, NV, 1))
    return wide[:NV] + crossed


def fine_kernel(
    face_ref, vec_ref, link_ref, site_ref, rhs_ref, table_ref, msg_ref,
    near_ref, field_ref, left_ref, time_ref, own_ref, block_ref, flat_ref, send_sem, recv_sem,
):
    sites = vec_ref.shape[-1]
    axes = ("gx", "gy", "gz")
    here = {name: lax.axis_index(name) for name in axes}

    def beside(mu, step):
        size = lax.axis_size(axes[mu])
        place = dict(here)
        place[axes[mu]] = (here[axes[mu]] + step + size) % size
        return (place["gz"], place["gy"], place["gx"])

    barrier = pltpu.get_barrier_semaphore()
    for mu in range(3):
        for step in (-1, 1):
            pl.semaphore_signal(
                barrier, inc=1, device_id=beside(mu, step), device_id_type=MESH
            )
    pl.semaphore_wait(barrier, 6)
    copies = []
    for mu in (0, 2, 1):
        for side, step in enumerate((-1, 1)):
            at = 2 * mu + side
            copies.append(
                pltpu.make_async_remote_copy(
                    src_ref=face_ref.at[at],
                    dst_ref=near_ref.at[at],
                    send_sem=send_sem.at[at],
                    recv_sem=recv_sem.at[at],
                    device_id=beside(mu, step),
                    device_id_type=MESH,
                )
            )
    for item in copies:
        item.start()

    position = lax.broadcasted_iota(jnp.int32, (NV, sites), 1)
    lane8 = lax.broadcasted_iota(jnp.int32, (8, LANES), 1)
    block_ref[NV:] = jnp.zeros((block_ref.shape[0] - NV, LANES), jnp.float32)

    @pl.loop(0, AT)
    def _(a):
        field_ref[...] = vec_ref[a].astype(jnp.float32)

        def value(part, spin, col):
            return field_ref[part * 12 + spin * 3 + col]

        left, right = [], []
        for chirality in range(2):
            for i in range(6):
                out_re, out_im = 0.0, 0.0
                for j in range(6):
                    at = chirality * 72 + i * 6 + j
                    m_re = site_ref[a, at : at + 1, :]
                    m_im = site_ref[a, at + 36 : at + 37, :]
                    v_re = field_ref[chirality * 6 + j]
                    v_im = field_ref[12 + chirality * 6 + j]
                    out_re = out_re + m_re * v_re - m_im * v_im
                    out_im = out_im + m_re * v_im + m_im * v_re
                right.append(stacked([out_re, out_im]))
                at = chirality * 6 + i
                left.append(stacked([field_ref[at], field_ref[12 + at]]))
        own = merged(across(jnp.concatenate(left, axis=1), jnp.concatenate(right, axis=1)))
        for mu in range(4):
            stride = site_strides[mu]
            last = position // stride % 4 == 3
            turned_minus, turned_plus, ahead_minus, ahead_plus, plain_minus, plain_plus = (
                [] for _ in range(6)
            )
            for col in range(3):
                turned = [[], []]
                for spin in range(4):
                    out_re, out_im = 0.0, 0.0
                    for row in range(3):
                        u_re = link(link_ref, a, mu, 0, row, col)
                        u_im = link(link_ref, a, mu, 1, row, col)
                        v_re, v_im = value(0, spin, row), value(1, spin, row)
                        out_re = out_re + u_re * v_re + u_im * v_im
                        out_im = out_im + u_re * v_im - u_im * v_re
                    turned[0].append(out_re)
                    turned[1].append(out_im)
                plain = [[value(part, spin, col) for spin in range(4)] for part in range(2)]
                ahead = [
                    [jnp.where(last, 0.0, pltpu.roll(item, sites - stride, 1)) for item in items]
                    for items in plain
                ]
                for spin in range(2):
                    turned_minus.append(stacked(halved(turned, mu, spin, -1)))
                    turned_plus.append(stacked(halved(turned, mu, spin, 1)))
                    ahead_minus.append(stacked(halved(ahead, mu, spin, -1)))
                    ahead_plus.append(stacked(halved(ahead, mu, spin, 1)))
                    plain_plus.append(stacked(halved(plain, mu, spin, 1)))
                    if mu == 3:
                        plain_minus.append(stacked(halved(plain, mu, spin, -1)))
            turned_minus = jnp.concatenate(turned_minus, axis=1)
            turned_plus = jnp.concatenate(turned_plus, axis=1)
            both = across(
                jnp.concatenate([turned_minus] + ahead_plus, axis=1),
                jnp.concatenate(ahead_minus + [turned_plus], axis=1),
            )
            own = own - 0.5 * merged(both)
            store_face(left_ref, (a, 2 * mu), packed(turned_minus, table_ref[mu, 1]))
            store_face(
                left_ref,
                (a, 2 * mu + 1),
                packed(jnp.concatenate(plain_plus, axis=1), table_ref[mu, 0]),
            )
            if mu == 3:
                store_face(
                    time_ref, (0, a), packed(jnp.concatenate(plain_minus, axis=1), table_ref[mu, 0])
                )
                store_face(time_ref, (1, a), packed(turned_plus, table_ref[mu, 1]))
        own_ref[a] = own * coarse_scale

    for item in copies:
        item.wait_recv()

    @pl.loop(0, AT)
    def _(a):
        for k in range(9):
            if k == 0:
                block = own_ref[a]
            else:
                mu, side = (k - 1) // 2, (k - 1) % 2
                if mu < 3:
                    near = near_ref[k - 1, a]
                else:
                    near = time_ref[side, (a + 1 + 2 * side) % AT]
                block = merged(across(left_ref[a, k - 1], near)) * (-0.5 * coarse_scale)
            block_ref[:NV] = rounded(block)
            pieces = [jnp.zeros((8, LANES), jnp.float32)] * 2
            for at in range(GROUP):
                rows = block_ref[pl.ds(at, 8, stride=GROUP), :]
                for part in range(2):
                    shift = (at - part) * NV % LANES
                    moved = rows if shift == 0 else pltpu.roll(rows, shift, 1)
                    pieces[part] = jnp.where(lane8 // NV == at, moved, pieces[part])
            for part in range(2):
                flat_ref[k, pl.ds(pl.multiple_of(a * 16 + part * 8, 8), 8), :] = pieces[part]

    for k in range(9):
        for chunk in range(CHUNKS):
            at = (k * CHUNKS + chunk) * LANES
            msg_ref[:, at : at + LANES] = flat_ref[k, pl.ds(chunk, ROWS, stride=8), :].astype(
                jnp.bfloat16
            )
    msg_ref[:, TILES * LANES :] = rhs_ref[...]
    for item in copies:
        item.wait_send()


def fine_message(vectors, links, site_term, rhs):
    sites = vectors.shape[-1]
    vec = jnp.transpose(vectors, (0, 2, 3, 4, 1, 5)).reshape(AT, 24, NV, sites)
    link_f = links.astype(jnp.float32).reshape(AT, 72, sites)
    site_f = site_term.astype(jnp.float32).reshape(AT, 144, sites)
    tiled = jnp.concatenate(
        [rhs.reshape(ROWS, NV)] * GROUP + [jnp.zeros((ROWS, LANES - GROUP * NV), rhs.dtype)], axis=1
    )
    table = face_table()
    face = (2 * NV, 3 * LANES)
    faces = pl.pallas_call(
        faces_kernel,
        grid=(AT,),
        in_specs=[
            pl.BlockSpec((1, 24, NV, sites), lambda a: (a, 0, 0, 0)),
            pl.BlockSpec((1, 72, sites), lambda a: (a, 0, 0)),
            pl.BlockSpec(table.shape, lambda a: (0, 0, 0, 0)),
        ],
        out_specs=pl.BlockSpec((6, 1) + face, lambda a: (0, a, 0, 0)),
        out_shape=jax.ShapeDtypeStruct((6, AT) + face, jnp.bfloat16),
        compiler_params=pltpu.CompilerParams(vmem_limit_bytes=32 << 20),
    )(vec, link_f, table)
    vmem = pl.BlockSpec(memory_space=pltpu.VMEM)
    return pl.pallas_call(
        fine_kernel,
        in_specs=[vmem] * 6,
        out_specs=vmem,
        out_shape=jax.ShapeDtypeStruct((ROWS, WIDE), jnp.bfloat16),
        scratch_shapes=[
            pltpu.VMEM((6, AT) + face, jnp.bfloat16),
            pltpu.VMEM((24, NV, sites), jnp.float32),
            pltpu.VMEM((AT, 8) + face, jnp.bfloat16),
            pltpu.VMEM((2, AT) + face, jnp.bfloat16),
            pltpu.VMEM((AT, NV, LANES), jnp.float32),
            pltpu.VMEM((8 * GROUP, LANES), jnp.float32),
            pltpu.VMEM((9, 8 * ROWS, LANES), jnp.float32),
            pltpu.SemaphoreType.DMA((6,)),
            pltpu.SemaphoreType.DMA((6,)),
        ],
        compiler_params=pltpu.CompilerParams(
            collective_id=2, has_side_effects=True, vmem_limit_bytes=32 << 20
        ),
    )(faces, vec, link_f, site_f, tiled, table)


def complex_mul(first, second):
    return (
        first[0] * second[0] - first[1] * second[1],
        first[0] * second[1] + first[1] * second[0],
    )


def rotate(top_entry, bottom_entry, scale_norm, upper_value, lower_value):
    conj_top = (top_entry[0], -top_entry[1])
    conj_bottom = (bottom_entry[0], -bottom_entry[1])
    part_one = complex_mul(conj_top, upper_value)
    part_two = complex_mul(conj_bottom, lower_value)
    part_three = complex_mul(bottom_entry, upper_value)
    part_four = complex_mul(top_entry, lower_value)
    new_upper = ((part_one[0] + part_two[0]) / scale_norm, (part_one[1] + part_two[1]) / scale_norm)
    new_lower = (
        (part_four[0] - part_three[0]) / scale_norm,
        (part_four[1] - part_three[1]) / scale_norm,
    )
    return (new_upper, new_lower)


def least_squares(hessen, beta):
    columns = len(hessen[0])
    zero_value = jnp.zeros((), jnp.float32)
    matrix = [list(row_list) for row_list in hessen]
    target = [(beta, zero_value)] + [(zero_value, zero_value)] * columns
    rotations = []
    for col_index in range(columns):
        for rot_index in range(col_index):
            top_entry, bottom_entry, scale_norm = rotations[rot_index]
            pair = rotate(
                top_entry,
                bottom_entry,
                scale_norm,
                matrix[rot_index][col_index],
                matrix[rot_index + 1][col_index],
            )
            matrix[rot_index][col_index] = pair[0]
            matrix[rot_index + 1][col_index] = pair[1]
        top_entry = matrix[col_index][col_index]
        bottom_entry = matrix[col_index + 1][col_index]
        scale_norm = jnp.sqrt(
            top_entry[0] * top_entry[0]
            + top_entry[1] * top_entry[1]
            + bottom_entry[0] * bottom_entry[0]
            + bottom_entry[1] * bottom_entry[1]
        )
        rotations.append((top_entry, bottom_entry, scale_norm))
        matrix[col_index][col_index] = (scale_norm, zero_value)
        matrix[col_index + 1][col_index] = (zero_value, zero_value)
        pair = rotate(top_entry, bottom_entry, scale_norm, target[col_index], target[col_index + 1])
        target[col_index] = pair[0]
        target[col_index + 1] = pair[1]
    weights = [None] * columns
    for row_index in reversed(range(columns)):
        remainder = target[row_index]
        for col_index in range(row_index + 1, columns):
            product_term = complex_mul(matrix[row_index][col_index], weights[col_index])
            remainder = (remainder[0] - product_term[0], remainder[1] - product_term[1])
        weights[row_index] = (
            remainder[0] / matrix[row_index][row_index][0],
            remainder[1] / matrix[row_index][row_index][0],
        )
    return weights


def split_two(value):
    high = value.astype(jnp.bfloat16)
    low = (value - high.astype(jnp.float32)).astype(jnp.bfloat16)
    return high, low


def gather_kernel(msg_ref, out_ref, chain_sem, plane_sem, cross_sem, core_sem, recv_sem, own_sem):
    size_z, size_y, size_x = (lax.axis_size(name) for name in ("gz", "gy", "gx"))
    z, y, x = (lax.axis_index(name) for name in ("gz", "gy", "gx"))
    middle = TILES // 2 * LANES
    spans = (pl.ds(0, middle), pl.ds(middle, WIDE - middle))

    def flipped(bits):
        low, high = z % 2, z // 2
        if bits & 1:
            low = 1 - low
        if bits & 2:
            high = 1 - high
        return high * 2 + low

    def slot(at_z, at_y, at_x):
        return (at_z * size_y + at_y) * size_x + at_x

    def copy(source, at, part, sem, target):
        return pltpu.make_async_remote_copy(
            src_ref=source.at[:, spans[part]],
            dst_ref=out_ref.at[at, :, spans[part]],
            send_sem=sem,
            recv_sem=recv_sem.at[at, part],
            device_id=target,
            device_id_type=MESH,
        )

    others = [(y + step) % size_y for step in range(1, size_y)]
    sides = ((x > 0, x - 1), (x < size_x - 1, x + 1))
    barrier = pltpu.get_barrier_semaphore()
    for bits in (1, 2):
        pl.semaphore_signal(
            barrier, inc=1, device_id=(flipped(bits), y, x), device_id_type=MESH
        )
    for other in others:
        pl.semaphore_signal(barrier, inc=1, device_id=(z, other, x), device_id_type=MESH)
    for exists, at in sides:

        @pl.when(exists)
        def _():
            pl.semaphore_signal(barrier, inc=1, device_id=(z, y, at), device_id_type=MESH)

    inner = (x > 0).astype(jnp.int32) + (x < size_x - 1).astype(jnp.int32)
    pl.semaphore_wait(barrier, 1 + size_y + inner)

    mine = slot(z, y, x)
    keep = pltpu.make_async_copy(msg_ref, out_ref.at[mine], own_sem)
    keep.start()

    def to_side(source, at_x, side, part):
        return copy(
            source, slot(z, y, at_x), part, chain_sem.at[side, at_x, part], (z, y, sides[side][1])
        )

    def to_plane(source, at_x, which, part):
        return copy(
            source,
            slot(z, y, at_x),
            part,
            plane_sem.at[which, at_x, part],
            (flipped(which + 1), y, x),
        )

    def to_cross(at_x, which):
        at = slot(flipped(which + 1), y, at_x)
        return copy(
            out_ref.at[at], at, which, cross_sem.at[which, at_x], (flipped(2 - which), y, x)
        )

    def to_core(source, bits, at_x, which, part):
        at = slot(flipped(bits), y, at_x)
        return copy(source, at, part, core_sem.at[which, bits, at_x, part], (z, others[which], x))

    def arrived(at, part):
        copy(out_ref.at[at], at, part, own_sem, (z, others[0], x)).wait_recv()

    def spread(source, at_x, toward):
        for part in range(2):
            for side in toward:

                @pl.when(sides[side][0])
                def _():
                    to_side(source, at_x, side, part).start()

            for which in range(2):
                to_plane(source, at_x, which, part).start()
            for which in range(len(others)):
                to_core(source, 0, at_x, which, part).start()

    def column(at_x, toward):
        at = slot(z, y, at_x)
        for part in range(2):
            arrived(at, part)
        spread(out_ref.at[at], at_x, toward)

    def next_plane(at_x):
        for which in range(2):
            at = slot(flipped(which + 1), y, at_x)
            for part in (which, 1 - which):
                arrived(at, part)
                if part == which:
                    to_cross(at_x, which).start()
                for other in range(len(others)):
                    to_core(out_ref.at[at], which + 1, at_x, other, part).start()

    def far_plane(at_x):
        at = slot(flipped(3), y, at_x)
        for part in range(2):
            arrived(at, part)
            for other in range(len(others)):
                to_core(out_ref.at[at], 3, at_x, other, part).start()

    def at_distance(distance, action):
        if distance == 0:
            action(x, None)
            return

        @pl.when(x >= distance)
        def _():
            action(x - distance, 1)

        @pl.when(x + distance < size_x)
        def _():
            action(x + distance, 0)

    spread(msg_ref, x, (0, 1))
    for distance in range(1, size_x + 2):
        if distance < size_x:
            at_distance(distance, lambda at_x, side: column(at_x, (side,)))
        if distance - 1 < size_x:
            at_distance(distance - 1, lambda at_x, side: next_plane(at_x))
        if 0 <= distance - 2 < size_x:
            at_distance(distance - 2, lambda at_x, side: far_plane(at_x))
    keep.wait()
    for at_x in range(size_x):
        for bits in range(4):
            for other in others:
                for part in range(2):
                    arrived(slot(flipped(bits), other, at_x), part)
    for at_x in range(size_x):
        for part in range(2):

            @pl.when((x > 0) & (x <= at_x))
            def _():
                to_side(msg_ref, at_x, 0, part).wait_send()

            @pl.when((x < size_x - 1) & (x >= at_x))
            def _():
                to_side(msg_ref, at_x, 1, part).wait_send()

            for which in range(2):
                to_plane(msg_ref, at_x, which, part).wait_send()
            for bits in range(4):
                for which in range(len(others)):
                    to_core(msg_ref, bits, at_x, which, part).wait_send()
        for which in range(2):
            to_cross(at_x, which).wait_send()


def gather_messages(message):
    size_z, size_y, size_x = (lax.axis_size(name) for name in ("gz", "gy", "gx"))
    assert size_z == 4
    devices = size_z * size_y * size_x
    dma = pltpu.SemaphoreType.DMA
    return pl.pallas_call(
        gather_kernel,
        out_shape=jax.ShapeDtypeStruct((devices, ROWS, WIDE), jnp.bfloat16),
        in_specs=[pl.BlockSpec(memory_space=pltpu.VMEM)],
        out_specs=pl.BlockSpec(memory_space=pltpu.VMEM),
        scratch_shapes=[
            dma((2, size_x, 2)),
            dma((2, size_x, 2)),
            dma((2, size_x)),
            dma((size_y - 1, 4, size_x, 2)),
            dma((devices, 2)),
            dma,
        ],
        compiler_params=pltpu.CompilerParams(
            collective_id=1, has_side_effects=True, vmem_limit_bytes=48 << 20
        ),
    )(message)


def total(value):
    return jnp.sum(jnp.sum(value, axis=0, keepdims=True), axis=1, keepdims=True)


def paired(value):
    row = lax.broadcasted_iota(jnp.int32, value.shape, 0)
    count = value.shape[0]
    return jnp.where(row % 2 == 0, pltpu.roll(value, count - 1, 0), pltpu.roll(value, 1, 0))


def gmres_kernel(sizes, pick_ref, rows_ref, reduce_ref, op_ref, sol_ref, acc_ref, one_ref, two_ref):
    size_z, size_y, size_x = sizes
    devices = size_z * size_y * size_x
    count = devices * ROWS
    row = lax.broadcasted_iota(jnp.int32, (count, LANES), 0)
    lane = lax.broadcasted_iota(jnp.int32, (count, LANES), 1)
    sign = jnp.where(row % 2 == 0, 1.0, -1.0)
    even8 = lax.broadcasted_iota(jnp.int32, (ROWS, LANES), 0) % 2 == 0
    lane8 = lax.broadcasted_iota(jnp.int32, (ROWS, LANES), 1)
    real = lane < NV

    def tile(ref, at):
        return ref[pl.ds(pl.multiple_of(at * ROWS, ROWS), ROWS), :]

    def apply(vector, swapped):
        one_ref[...] = vector * sign
        two_ref[...] = swapped

        @pl.loop(0, devices)
        def _(at):
            x = at % size_x
            y = at // size_x % size_y
            z = at // (size_x * size_y)

            def slot(at_z, at_y, at_x):
                return (at_z * size_y + at_y) * size_x + at_x

            places = (
                slot(z, y, (x + 1) % size_x),
                slot(z, y, (x + size_x - 1) % size_x),
                slot(z, (y + 1) % size_y, x),
                slot(z, (y + size_y - 1) % size_y, x),
                slot((z + 1) % size_z, y, x),
                slot((z + size_z - 1) % size_z, y, x),
            )
            near = []
            for ref in (one_ref, two_ref):
                own = tile(ref, at)
                near.append(
                    [own]
                    + [tile(ref, place) for place in places]
                    + [pltpu.roll(own, ROWS - 2, 0), pltpu.roll(own, 2, 0)]
                )
            for chunk in range(CHUNKS):
                sums = [0.0, 0.0]
                for k in range(9):
                    start = (k * CHUNKS + chunk) * LANES
                    rows = rows_ref[at, :, start : start + LANES].astype(jnp.float32)
                    for part in range(2):
                        sums[part] = sums[part] + rows * near[part][k]
                acc_ref[
                    pl.ds(pl.multiple_of(at * ROWS, ROWS), ROWS), chunk * LANES : (chunk + 1) * LANES
                ] = jnp.where(
                    even8,
                    sums[0] + pltpu.roll(sums[0], ROWS - 1, 0),
                    sums[1] + pltpu.roll(sums[1], 1, 0),
                )

        high, low = split_two(acc_ref[...])
        return jnp.dot(high, reduce_ref[...], preferred_element_type=jnp.float32) + jnp.dot(
            low, reduce_ref[...], preferred_element_type=jnp.float32
        )

    for z in range(size_z):
        for y in range(size_y):
            for x in range(size_x):
                at = (z * size_y + y) * size_x + x
                place = (z * size_x + x) * size_y + y
                chosen = pick_ref[at]

                @pl.when(chosen < 0)
                def _():
                    op_ref[place] = jnp.zeros(op_ref.shape[1:], op_ref.dtype)

                @pl.when(chosen >= 0)
                def _():
                    shift = (ROWS - 2 * chosen) % ROWS
                    for k in range(9):
                        turned = []
                        for chunk in range(CHUNKS):
                            start = (k * CHUNKS + chunk) * LANES
                            rows = rows_ref[at, :, start : start + LANES].astype(jnp.float32)
                            rows = pltpu.roll(rows, shift, 0)
                            back = chunk * (LANES - GROUP * NV)
                            turned.append(rows if back == 0 else pltpu.roll(rows, LANES - back, 1))
                        for chunk in range(CHUNKS):
                            start = chunk * LANES
                            width = min(LANES, NV * NV - start)
                            value = turned[chunk]
                            if chunk + 1 < CHUNKS:
                                cut = GROUP * NV - chunk * (LANES - GROUP * NV)
                                value = jnp.where(lane8 < cut, value, turned[chunk + 1])
                            op_ref[place, k, :, start : start + width] = value[:2, :width].astype(
                                jnp.bfloat16
                            )

    right_side = rows_ref[:, :, TILES * LANES :].astype(jnp.float32).reshape(count, LANES)
    zero_value = jnp.zeros((1, 1), jnp.float32)

    def squares(value):
        return total(jnp.where(real, value * value, 0.0))

    beta = jnp.sqrt(squares(right_side) + epsilon)
    basis = [right_side / beta]
    swapped = [paired(basis[0])]
    hessen = []
    for row_index in range(ITERS + 1):
        hessen.append([(zero_value, zero_value)] * ITERS)
    for column in range(ITERS):
        work = apply(basis[column], swapped[column])
        for row_index in range(column + 1):
            turned = swapped[row_index] * sign
            coef_re = total(jnp.where(real, basis[row_index] * work, 0.0))
            coef_im = -total(jnp.where(real, turned * work, 0.0))
            hessen[row_index][column] = (coef_re, coef_im)
            work = work - coef_re * basis[row_index] + coef_im * turned
        norm_now = jnp.sqrt(squares(work) + epsilon)
        hessen[column + 1][column] = (norm_now, zero_value)
        if column + 1 < ITERS:
            basis.append(work / norm_now)
            swapped.append(paired(basis[-1]))
    weights = least_squares(hessen, beta)
    answer = jnp.zeros_like(right_side)
    for column in range(ITERS):
        answer = (
            answer
            + weights[column][0] * basis[column]
            - weights[column][1] * (swapped[column] * sign)
        )
    one_ref[...] = answer
    for z in range(size_z):
        for y in range(size_y):
            for x in range(size_x):
                at = (z * size_y + y) * size_x + x
                chosen = pick_ref[at]
                shift = (ROWS - 2 * jnp.maximum(chosen, 0)) % ROWS
                rows = pltpu.roll(one_ref[at * ROWS : (at + 1) * ROWS], shift, 0)
                rows = jnp.where(chosen >= 0, rows, 0.0)
                sol_ref[(z * size_x + x) * size_y + y] = rows[:2, :NV]


def reduce_table():
    table = np.zeros((CHUNKS, LANES, LANES), np.float32)
    for chunk in range(CHUNKS):
        for at in range(GROUP):
            out = chunk * GROUP + at
            if out < NV:
                for copy in range(GROUP):
                    table[chunk, at * NV : (at + 1) * NV, copy * NV + out] = 1.0
    return table.reshape(CHUNKS * LANES, LANES).astype(jnp.bfloat16)


def coarse_solve(rows, owner):
    sizes = tuple(lax.axis_size(name) for name in ("gz", "gy", "gx"))
    devices, count = rows.shape[0], rows.shape[0] * ROWS
    mine = owner.reshape(-1, AT) == lax.axis_index(("gz", "gx"))
    chosen = jnp.max(jnp.where(mine, jnp.arange(AT, dtype=jnp.int32), -1), axis=1)
    vmem = pl.BlockSpec(memory_space=pltpu.VMEM)
    return pl.pallas_call(
        lambda *refs: gmres_kernel(sizes, *refs),
        out_shape=(
            jax.ShapeDtypeStruct((devices, 9, 2, NV * NV), jnp.bfloat16),
            jax.ShapeDtypeStruct((devices, 2, NV), jnp.float32),
        ),
        in_specs=[pl.BlockSpec(memory_space=pltpu.SMEM), vmem, vmem],
        out_specs=[vmem, vmem],
        scratch_shapes=[
            pltpu.VMEM((count, CHUNKS * LANES), jnp.float32),
            pltpu.VMEM((count, LANES), jnp.float32),
            pltpu.VMEM((count, LANES), jnp.float32),
        ],
        compiler_params=pltpu.CompilerParams(vmem_limit_bytes=60 << 20),
    )(chosen, rows, reduce_table())


def on_device(vectors, links, site_term, owner, coarse_rhs):
    message = fine_message(
        vectors[0, 0, 0], links[0, 0, 0], site_term[0, 0, 0], coarse_rhs[0, 0, 0]
    )
    rows = gather_messages(message)
    operator, answer = coarse_solve(rows, owner)
    return operator[None], answer[None]


def solution(mesh):
    return jax.shard_map(
        on_device,
        mesh=mesh,
        in_specs=(
            P("gz", "gy", "gx", None, None, None, None, None, None),
            P("gz", "gy", "gx", None, None, None, None, None, None),
            P("gz", "gy", "gx", None, None, None, None, None, None),
            P(),
            P("gz", "gy", "gx", None, None, None),
        ),
        out_specs=(P(("gz", "gx"), None, None, None, None), P(("gz", "gx"), None, None, None)),
        check_vma=False,
    )
```

```python
import jax
import jax.numpy as jnp
import numpy as np
from jax import lax
from jax.experimental import pallas as pl
from jax.experimental.pallas import tpu as pltpu
from jax.sharding import PartitionSpec as P

NV = 24
AT = 4
ITERS = 4
PAIR = 1
LANES = 128
GROUP = LANES // NV
CHUNKS = -(-NV // GROUP)
ROWS = 2 * AT
TILES = 9 * CHUNKS
WIDE = (TILES + 1) * LANES
MESH = pl.DeviceIdType.MESH


coarse_scale = 1.0 / 256.0
epsilon = 1e-06
site_strides = (64, 16, 4, 1)
lower_table = (
    (((1, 3, 1), (0, 3, -1)), ((1, 2, 1), (0, 2, -1))),
    (((0, 3, -1), (1, 3, -1)), ((0, 2, 1), (1, 2, 1))),
    (((1, 2, 1), (0, 2, -1)), ((1, 3, -1), (0, 3, 1))),
    (((0, 2, 1), (1, 2, 1)), ((0, 3, 1), (1, 3, 1))),
)


def rounded(value):
    return value.astype(jnp.bfloat16).astype(jnp.float32)


def face_table(stride, layer):
    row = lax.broadcasted_iota(jnp.int32, (512, LANES), 0)
    lane = lax.broadcasted_iota(jnp.int32, (512, LANES), 1)
    place = lane % 64
    site = place // stride * 4 * stride + place % stride + 3 * layer * stride
    return jnp.where(row == site + lane // 64 * 256, 1.0, 0.0).astype(jnp.bfloat16)


def halved(field, direction, spin, sign):
    pair = []
    for part in range(2):
        from_part, from_spin, factor = lower_table[direction][spin][part]
        lower = field[from_part][from_spin]
        upper = field[part][spin]
        pair.append(upper + lower if sign * factor > 0 else upper - lower)
    return pair


def link(link_ref, direction, part, row, col):
    index = (direction * 9 + row * 3 + col) * 2 + part
    return link_ref[index : index + 1, :]


def stacked(pieces):
    return jnp.concatenate(pieces, axis=0).astype(jnp.bfloat16)


def across(left, right):
    return lax.dot_general(
        left, right, (((1,), (1,)), ((), ())), preferred_element_type=jnp.float32
    )


def packed(operand, table):
    rows = jnp.concatenate([operand[:, at * 512 : (at + 1) * 512] for at in range(3)], axis=0)
    out = jnp.dot(rows, table, preferred_element_type=jnp.float32)
    return [out[at * 2 * NV : (at + 1) * 2 * NV] for at in range(3)]


def store_face(ref, index, pieces):
    for at, piece in enumerate(pieces):
        ref[index + (slice(None), slice(at * LANES, (at + 1) * LANES))] = piece.astype(jnp.bfloat16)


def faces_kernel(vec_ref, link_ref, face_ref, table_ref, row_ref):
    @pl.when(pl.program_id(0) == 0)
    def _():
        for mu in range(3):
            for layer in range(2):
                table_ref[mu, layer] = face_table(site_strides[mu], layer)

    field = [
        [
            [vec_ref[0, part * 12 + spin * 3 + col].astype(jnp.float32) for spin in range(4)]
            for part in range(2)
        ]
        for col in range(3)
    ]
    for mu in range(3):
        sides = []
        for sign in (-1, 1):
            pieces = []
            for col in range(3):
                for spin in range(2):
                    pieces.append(stacked(halved(field[col], mu, spin, sign)))
            sides.append(jnp.concatenate(pieces, axis=1))
        store_face(face_ref, (2 * mu, 0), packed(sides[0], table_ref[mu, 0]))
        plus = packed(sides[1], table_ref[mu, 1])
        for row in range(3):
            for col in range(3):
                at = (row * 3 + col) * 2
                row_ref[mu, at : at + 2] = link_ref[0, mu, row, col].astype(jnp.float32)
        rows = row_ref[mu].astype(jnp.bfloat16)
        links = jnp.dot(
            rows, table_ref[mu, 1, :256], preferred_element_type=jnp.float32
        ) + jnp.dot(rows, table_ref[mu, 1, 256:], preferred_element_type=jnp.float32)
        back = []
        for col in range(3):
            out_re, out_im = 0.0, 0.0
            for row in range(3):
                at = (row * 3 + col) * 2
                u_re, u_im = links[at : at + 1], links[at + 1 : at + 2]
                p_re, p_im = plus[row][:NV], plus[row][NV:]
                out_re = out_re + u_re * p_re + u_im * p_im
                out_im = out_im + u_re * p_im - u_im * p_re
            back.append(jnp.concatenate([out_re, out_im], axis=0))
        store_face(face_ref, (2 * mu + 1, 0), back)


def merged(product):
    lane = lax.broadcasted_iota(jnp.int32, (NV, LANES), 1)
    wide = jnp.concatenate([product, jnp.zeros((2 * NV, LANES - 2 * NV), jnp.float32)], axis=1)
    low = wide[NV:]
    crossed = jnp.where(lane < NV, pltpu.roll(low, LANES - NV, 1), -pltpu.roll(low, NV, 1))
    return wide[:NV] + crossed


def fine_kernel(
    face_ref, vec_ref, raw_link_ref, raw_site_ref, rhs_ref, msg_ref,
    near_ref, field_ref, left_ref, time_ref, own_ref, block_ref, flat_ref,
    table_ref, link_ref, site_ref, side_ref, send_sem, recv_sem,
):
    sites = vec_ref.shape[-1]
    axes = ("gx", "gy", "gz")
    here = {name: lax.axis_index(name) for name in axes}

    def beside(mu, step):
        size = lax.axis_size(axes[mu])
        place = dict(here)
        place[axes[mu]] = (here[axes[mu]] + step + size) % size
        return (place["gz"], place["gy"], place["gx"])

    barrier = pltpu.get_barrier_semaphore()
    for mu in range(3):
        for step in (-1, 1):
            pl.semaphore_signal(
                barrier, inc=1, device_id=beside(mu, step), device_id_type=MESH
            )
    pl.semaphore_wait(barrier, 6)
    copies = []
    for mu in (0, 2, 1):
        for side, step in enumerate((-1, 1)):
            at = 2 * mu + side
            copies.append(
                pltpu.make_async_remote_copy(
                    src_ref=face_ref.at[at],
                    dst_ref=near_ref.at[at],
                    send_sem=send_sem.at[at],
                    recv_sem=recv_sem.at[at],
                    device_id=beside(mu, step),
                    device_id_type=MESH,
                )
            )
    for item in copies:
        item.start()

    position = lax.broadcasted_iota(jnp.int32, (NV, sites), 1)
    lane8 = lax.broadcasted_iota(jnp.int32, (8, LANES), 1)
    block_ref[NV:] = jnp.zeros((block_ref.shape[0] - NV, LANES), jnp.float32)
    for mu in range(4):
        for layer in range(2):
            table_ref[mu, layer] = face_table(site_strides[mu], layer)

    @pl.loop(0, AT)
    def _(a):
        field_ref[...] = vec_ref[a].astype(jnp.float32)
        for at in range(36):
            mu, row, col = at // 9, at // 3 % 3, at % 3
            link_ref[2 * at : 2 * at + 2] = raw_link_ref[a, mu, row, col].astype(jnp.float32)
        for at in range(72):
            chirality, row, col = at // 36, at // 6 % 6, at % 6
            site_ref[2 * at : 2 * at + 2] = raw_site_ref[a, chirality, row, col].astype(jnp.float32)

        def value(part, spin, col):
            return field_ref[part * 12 + spin * 3 + col]

        left, right = [], []
        for chirality in range(2):
            for i in range(6):
                out_re, out_im = 0.0, 0.0
                for j in range(6):
                    at = (chirality * 36 + i * 6 + j) * 2
                    m_re = site_ref[at : at + 1, :]
                    m_im = site_ref[at + 1 : at + 2, :]
                    v_re = field_ref[chirality * 6 + j]
                    v_im = field_ref[12 + chirality * 6 + j]
                    out_re = out_re + m_re * v_re - m_im * v_im
                    out_im = out_im + m_re * v_im + m_im * v_re
                right.append(stacked([out_re, out_im]))
                at = chirality * 6 + i
                left.append(stacked([field_ref[at], field_ref[12 + at]]))
        own = merged(across(jnp.concatenate(left, axis=1), jnp.concatenate(right, axis=1)))
        for mu in range(4):
            stride = site_strides[mu]
            last = position // stride % 4 == 3
            turned_minus, turned_plus, ahead_minus, ahead_plus, plain_minus, plain_plus = (
                [] for _ in range(6)
            )
            for col in range(3):
                turned = [[], []]
                for spin in range(4):
                    out_re, out_im = 0.0, 0.0
                    for row in range(3):
                        u_re = link(link_ref, mu, 0, row, col)
                        u_im = link(link_ref, mu, 1, row, col)
                        v_re, v_im = value(0, spin, row), value(1, spin, row)
                        out_re = out_re + u_re * v_re + u_im * v_im
                        out_im = out_im + u_re * v_im - u_im * v_re
                    turned[0].append(out_re)
                    turned[1].append(out_im)
                plain = [[value(part, spin, col) for spin in range(4)] for part in range(2)]
                ahead = [
                    [jnp.where(last, 0.0, pltpu.roll(item, sites - stride, 1)) for item in items]
                    for items in plain
                ]
                for spin in range(2):
                    turned_minus.append(stacked(halved(turned, mu, spin, -1)))
                    turned_plus.append(stacked(halved(turned, mu, spin, 1)))
                    ahead_minus.append(stacked(halved(ahead, mu, spin, -1)))
                    ahead_plus.append(stacked(halved(ahead, mu, spin, 1)))
                    plain_plus.append(stacked(halved(plain, mu, spin, 1)))
                    if mu == 3:
                        plain_minus.append(stacked(halved(plain, mu, spin, -1)))
            turned_minus = jnp.concatenate(turned_minus, axis=1)
            turned_plus = jnp.concatenate(turned_plus, axis=1)
            both = across(
                jnp.concatenate([turned_minus] + ahead_plus, axis=1),
                jnp.concatenate(ahead_minus + [turned_plus], axis=1),
            )
            own = own - 0.5 * merged(both)
            store_face(left_ref, (a, 2 * mu), packed(turned_minus, table_ref[mu, 1]))
            store_face(
                left_ref,
                (a, 2 * mu + 1),
                packed(jnp.concatenate(plain_plus, axis=1), table_ref[mu, 0]),
            )
            if mu == 3:
                store_face(
                    time_ref, (0, a), packed(jnp.concatenate(plain_minus, axis=1), table_ref[mu, 0])
                )
                store_face(time_ref, (1, a), packed(turned_plus, table_ref[mu, 1]))
        own_ref[a] = own * coarse_scale

    for item in copies:
        item.wait_recv()

    @pl.loop(0, AT)
    def _(a):
        for k in range(9):
            if k == 0:
                block = own_ref[a]
            else:
                mu, side = (k - 1) // 2, (k - 1) % 2
                if mu < 3:
                    near = near_ref[k - 1, a]
                else:
                    near = time_ref[side, (a + 1 + 2 * side) % AT]
                block = merged(across(left_ref[a, k - 1], near)) * (-0.5 * coarse_scale)
            block_ref[:NV] = rounded(block)
            pieces = [jnp.zeros((8, LANES), jnp.float32)] * 2
            for at in range(GROUP):
                rows = block_ref[pl.ds(at, 8, stride=GROUP), :]
                for part in range(2):
                    shift = (at - part) * NV % LANES
                    moved = rows if shift == 0 else pltpu.roll(rows, shift, 1)
                    pieces[part] = jnp.where(lane8 // NV == at, moved, pieces[part])
            for part in range(2):
                flat_ref[k, pl.ds(pl.multiple_of(a * 16 + part * 8, 8), 8), :] = pieces[part]

    for k in range(9):
        for chunk in range(CHUNKS):
            at = (k * CHUNKS + chunk) * LANES
            msg_ref[:, at : at + LANES] = flat_ref[k, pl.ds(chunk, ROWS, stride=8), :].astype(
                jnp.bfloat16
            )
    for a in range(AT):
        rhs = rhs_ref[a].astype(jnp.float32)
        side_ref[2 * a : 2 * a + 2] = jnp.concatenate(
            [rhs] * GROUP + [jnp.zeros((2, LANES - GROUP * NV), jnp.float32)], axis=1
        )
    msg_ref[:, TILES * LANES :] = side_ref[...].astype(jnp.bfloat16)
    for item in copies:
        item.wait_send()


def fine_message(vectors, links, site_term, rhs):
    sites = vectors.shape[-1]
    vec = jnp.transpose(vectors, (0, 2, 3, 4, 1, 5)).reshape(AT, 24, NV, sites)
    link_rows = jnp.transpose(links, (0, 1, 3, 4, 2, 5))
    site_rows = jnp.transpose(site_term, (0, 1, 3, 4, 2, 5))
    face = (2 * NV, 3 * LANES)
    faces = pl.pallas_call(
        faces_kernel,
        grid=(AT,),
        in_specs=[
            pl.BlockSpec((1, 24, NV, sites), lambda a: (a, 0, 0, 0)),
            pl.BlockSpec((1, 4, 3, 3, 2, sites), lambda a: (a, 0, 0, 0, 0, 0)),
        ],
        out_specs=pl.BlockSpec((6, 1) + face, lambda a: (0, a, 0, 0)),
        out_shape=jax.ShapeDtypeStruct((6, AT) + face, jnp.bfloat16),
        scratch_shapes=[
            pltpu.VMEM((3, 2, 512, LANES), jnp.bfloat16),
            pltpu.VMEM((3, 18, sites), jnp.float32),
        ],
        compiler_params=pltpu.CompilerParams(vmem_limit_bytes=24 << 20),
    )(vec, link_rows)
    vmem = pl.BlockSpec(memory_space=pltpu.VMEM)
    return pl.pallas_call(
        fine_kernel,
        in_specs=[vmem] * 5,
        out_specs=vmem,
        out_shape=jax.ShapeDtypeStruct((ROWS, WIDE), jnp.bfloat16),
        scratch_shapes=[
            pltpu.VMEM((6, AT) + face, jnp.bfloat16),
            pltpu.VMEM((24, NV, sites), jnp.float32),
            pltpu.VMEM((AT, 8) + face, jnp.bfloat16),
            pltpu.VMEM((2, AT) + face, jnp.bfloat16),
            pltpu.VMEM((AT, NV, LANES), jnp.float32),
            pltpu.VMEM((8 * GROUP, LANES), jnp.float32),
            pltpu.VMEM((9, 8 * ROWS, LANES), jnp.float32),
            pltpu.VMEM((4, 2, 512, LANES), jnp.bfloat16),
            pltpu.VMEM((72, sites), jnp.float32),
            pltpu.VMEM((144, sites), jnp.float32),
            pltpu.VMEM((ROWS, LANES), jnp.float32),
            pltpu.SemaphoreType.DMA((6,)),
            pltpu.SemaphoreType.DMA((6,)),
        ],
        compiler_params=pltpu.CompilerParams(
            collective_id=2, has_side_effects=True, vmem_limit_bytes=32 << 20
        ),
    )(faces, vec, link_rows, site_rows, rhs)


def complex_mul(first, second):
    return (
        first[0] * second[0] - first[1] * second[1],
        first[0] * second[1] + first[1] * second[0],
    )


def rotate(top_entry, bottom_entry, scale_norm, upper_value, lower_value):
    conj_top = (top_entry[0], -top_entry[1])
    conj_bottom = (bottom_entry[0], -bottom_entry[1])
    part_one = complex_mul(conj_top, upper_value)
    part_two = complex_mul(conj_bottom, lower_value)
    part_three = complex_mul(bottom_entry, upper_value)
    part_four = complex_mul(top_entry, lower_value)
    new_upper = ((part_one[0] + part_two[0]) / scale_norm, (part_one[1] + part_two[1]) / scale_norm)
    new_lower = (
        (part_four[0] - part_three[0]) / scale_norm,
        (part_four[1] - part_three[1]) / scale_norm,
    )
    return (new_upper, new_lower)


def least_squares(hessen, beta):
    columns = len(hessen[0])
    zero_value = jnp.zeros((), jnp.float32)
    matrix = [list(row_list) for row_list in hessen]
    target = [(beta, zero_value)] + [(zero_value, zero_value)] * columns
    rotations = []
    for col_index in range(columns):
        for rot_index in range(col_index):
            top_entry, bottom_entry, scale_norm = rotations[rot_index]
            pair = rotate(
                top_entry,
                bottom_entry,
                scale_norm,
                matrix[rot_index][col_index],
                matrix[rot_index + 1][col_index],
            )
            matrix[rot_index][col_index] = pair[0]
            matrix[rot_index + 1][col_index] = pair[1]
        top_entry = matrix[col_index][col_index]
        bottom_entry = matrix[col_index + 1][col_index]
        scale_norm = jnp.sqrt(
            top_entry[0] * top_entry[0]
            + top_entry[1] * top_entry[1]
            + bottom_entry[0] * bottom_entry[0]
            + bottom_entry[1] * bottom_entry[1]
        )
        rotations.append((top_entry, bottom_entry, scale_norm))
        matrix[col_index][col_index] = (scale_norm, zero_value)
        matrix[col_index + 1][col_index] = (zero_value, zero_value)
        pair = rotate(top_entry, bottom_entry, scale_norm, target[col_index], target[col_index + 1])
        target[col_index] = pair[0]
        target[col_index + 1] = pair[1]
    weights = [None] * columns
    for row_index in reversed(range(columns)):
        remainder = target[row_index]
        for col_index in range(row_index + 1, columns):
            product_term = complex_mul(matrix[row_index][col_index], weights[col_index])
            remainder = (remainder[0] - product_term[0], remainder[1] - product_term[1])
        weights[row_index] = (
            remainder[0] / matrix[row_index][row_index][0],
            remainder[1] / matrix[row_index][row_index][0],
        )
    return weights


def split_two(value):
    high = value.astype(jnp.bfloat16)
    low = (value - high.astype(jnp.float32)).astype(jnp.bfloat16)
    return high, low


def gather_kernel(msg_ref, out_ref, chain_sem, plane_sem, cross_sem, core_sem, recv_sem, own_sem):
    size_z, size_y, size_x = (lax.axis_size(name) for name in ("gz", "gy", "gx"))
    z, y, x = (lax.axis_index(name) for name in ("gz", "gy", "gx"))
    middle = TILES // 2 * LANES
    spans = (pl.ds(0, middle), pl.ds(middle, WIDE - middle))

    def flipped(bits):
        low, high = z % 2, z // 2
        if bits & 1:
            low = 1 - low
        if bits & 2:
            high = 1 - high
        return high * 2 + low

    def slot(at_z, at_y, at_x):
        return (at_z * size_y + at_y) * size_x + at_x

    def copy(source, at, part, sem, target):
        return pltpu.make_async_remote_copy(
            src_ref=source.at[:, spans[part]],
            dst_ref=out_ref.at[at, :, spans[part]],
            send_sem=sem,
            recv_sem=recv_sem.at[at, part],
            device_id=target,
            device_id_type=MESH,
        )

    others = [(y + step) % size_y for step in range(1, size_y)]
    sides = ((x > 0, x - 1), (x < size_x - 1, x + 1))
    barrier = pltpu.get_barrier_semaphore()
    for bits in (1, 2):
        pl.semaphore_signal(
            barrier, inc=1, device_id=(flipped(bits), y, x), device_id_type=MESH
        )
    for other in others:
        pl.semaphore_signal(barrier, inc=1, device_id=(z, other, x), device_id_type=MESH)
    for exists, at in sides:

        @pl.when(exists)
        def _():
            pl.semaphore_signal(barrier, inc=1, device_id=(z, y, at), device_id_type=MESH)

    inner = (x > 0).astype(jnp.int32) + (x < size_x - 1).astype(jnp.int32)
    pl.semaphore_wait(barrier, 1 + size_y + inner)

    mine = slot(z, y, x)
    keep = pltpu.make_async_copy(msg_ref, out_ref.at[mine], own_sem)
    keep.start()

    def to_side(source, at_x, side, part):
        return copy(
            source, slot(z, y, at_x), part, chain_sem.at[side, at_x, part], (z, y, sides[side][1])
        )

    def to_plane(source, at_x, which, part):
        return copy(
            source,
            slot(z, y, at_x),
            part,
            plane_sem.at[which, at_x, part],
            (flipped(which + 1), y, x),
        )

    def to_cross(at_x, which):
        at = slot(flipped(which + 1), y, at_x)
        return copy(
            out_ref.at[at], at, which, cross_sem.at[which, at_x], (flipped(2 - which), y, x)
        )

    def to_core(source, bits, at_x, which, part):
        at = slot(flipped(bits), y, at_x)
        return copy(source, at, part, core_sem.at[which, bits, at_x, part], (z, others[which], x))

    def arrived(at, part):
        copy(out_ref.at[at], at, part, own_sem, (z, others[0], x)).wait_recv()

    def spread(source, at_x, toward):
        for part in range(2):
            for side in toward:

                @pl.when(sides[side][0])
                def _():
                    to_side(source, at_x, side, part).start()

            for which in range(2):
                to_plane(source, at_x, which, part).start()
            for which in range(len(others)):
                to_core(source, 0, at_x, which, part).start()

    def column(at_x, toward):
        at = slot(z, y, at_x)
        for part in range(2):
            arrived(at, part)
        spread(out_ref.at[at], at_x, toward)

    def next_plane(at_x):
        for which in range(2):
            at = slot(flipped(which + 1), y, at_x)
            for part in (which, 1 - which):
                arrived(at, part)
                if part == which:
                    to_cross(at_x, which).start()
                for other in range(len(others)):
                    to_core(out_ref.at[at], which + 1, at_x, other, part).start()

    def far_plane(at_x):
        at = slot(flipped(3), y, at_x)
        for part in range(2):
            arrived(at, part)
            for other in range(len(others)):
                to_core(out_ref.at[at], 3, at_x, other, part).start()

    def at_distance(distance, action):
        if distance == 0:
            action(x, None)
            return

        @pl.when(x >= distance)
        def _():
            action(x - distance, 1)

        @pl.when(x + distance < size_x)
        def _():
            action(x + distance, 0)

    spread(msg_ref, x, (0, 1))
    for distance in range(1, size_x + 2):
        if distance < size_x:
            at_distance(distance, lambda at_x, side: column(at_x, (side,)))
        if distance - 1 < size_x:
            at_distance(distance - 1, lambda at_x, side: next_plane(at_x))
        if 0 <= distance - 2 < size_x:
            at_distance(distance - 2, lambda at_x, side: far_plane(at_x))
    keep.wait()
    for at_x in range(size_x):
        for bits in range(4):
            for other in others:
                for part in range(2):
                    arrived(slot(flipped(bits), other, at_x), part)
    for at_x in range(size_x):
        for part in range(2):

            @pl.when((x > 0) & (x <= at_x))
            def _():
                to_side(msg_ref, at_x, 0, part).wait_send()

            @pl.when((x < size_x - 1) & (x >= at_x))
            def _():
                to_side(msg_ref, at_x, 1, part).wait_send()

            for which in range(2):
                to_plane(msg_ref, at_x, which, part).wait_send()
            for bits in range(4):
                for which in range(len(others)):
                    to_core(msg_ref, bits, at_x, which, part).wait_send()
        for which in range(2):
            to_cross(at_x, which).wait_send()


def gather_messages(message):
    size_z, size_y, size_x = (lax.axis_size(name) for name in ("gz", "gy", "gx"))
    assert size_z == 4
    devices = size_z * size_y * size_x
    dma = pltpu.SemaphoreType.DMA
    return pl.pallas_call(
        gather_kernel,
        out_shape=jax.ShapeDtypeStruct((devices, ROWS, WIDE), jnp.bfloat16),
        in_specs=[pl.BlockSpec(memory_space=pltpu.VMEM)],
        out_specs=pl.BlockSpec(memory_space=pltpu.VMEM),
        scratch_shapes=[
            dma((2, size_x, 2)),
            dma((2, size_x, 2)),
            dma((2, size_x)),
            dma((size_y - 1, 4, size_x, 2)),
            dma((devices, 2)),
            dma,
        ],
        compiler_params=pltpu.CompilerParams(
            collective_id=1, has_side_effects=True, vmem_limit_bytes=48 << 20
        ),
    )(message)


def total(value):
    return jnp.sum(jnp.sum(value, axis=0, keepdims=True), axis=1, keepdims=True)


def paired(value):
    row = lax.broadcasted_iota(jnp.int32, value.shape, 0)
    count = value.shape[0]
    return jnp.where(row % 2 == 0, pltpu.roll(value, count - 1, 0), pltpu.roll(value, 1, 0))


def gmres_kernel(
    owner_ref, rows_ref, reduce_ref, op_ref, sol_ref, acc_ref, one_ref, two_ref, out_ref
):
    size_z, size_y, size_x = owner_ref.shape[:3]
    me = lax.axis_index("gz") * size_x + lax.axis_index("gx")
    devices = size_z * size_y * size_x
    count = devices * ROWS
    row = lax.broadcasted_iota(jnp.int32, (count, LANES), 0)
    lane = lax.broadcasted_iota(jnp.int32, (count, LANES), 1)
    sign = jnp.where(row % 2 == 0, 1.0, -1.0)
    even8 = lax.broadcasted_iota(jnp.int32, (ROWS, LANES), 0) % 2 == 0
    lane8 = lax.broadcasted_iota(jnp.int32, (ROWS, LANES), 1)
    real = lane < NV

    def tile(ref, at):
        return ref[pl.ds(pl.multiple_of(at * ROWS, ROWS), ROWS), :]

    def apply(vector, swapped):
        one_ref[...] = vector * sign
        two_ref[...] = swapped

        @pl.loop(0, devices)
        def _(at):
            x = at % size_x
            y = at // size_x % size_y
            z = at // (size_x * size_y)

            def slot(at_z, at_y, at_x):
                return (at_z * size_y + at_y) * size_x + at_x

            places = (
                slot(z, y, (x + 1) % size_x),
                slot(z, y, (x + size_x - 1) % size_x),
                slot(z, (y + 1) % size_y, x),
                slot(z, (y + size_y - 1) % size_y, x),
                slot((z + 1) % size_z, y, x),
                slot((z + size_z - 1) % size_z, y, x),
            )
            near = []
            for ref in (one_ref, two_ref):
                own = tile(ref, at)
                near.append(
                    [own]
                    + [tile(ref, place) for place in places]
                    + [pltpu.roll(own, ROWS - 2, 0), pltpu.roll(own, 2, 0)]
                )
            for chunk in range(CHUNKS):
                sums = [0.0, 0.0]
                for k in range(9):
                    start = (k * CHUNKS + chunk) * LANES
                    rows = rows_ref[at, :, start : start + LANES].astype(jnp.float32)
                    for part in range(2):
                        sums[part] = sums[part] + rows * near[part][k]
                acc_ref[
                    pl.ds(pl.multiple_of(at * ROWS, ROWS), ROWS), chunk * LANES : (chunk + 1) * LANES
                ] = jnp.where(
                    even8,
                    sums[0] + pltpu.roll(sums[0], ROWS - 1, 0),
                    sums[1] + pltpu.roll(sums[1], 1, 0),
                )

        high, low = split_two(acc_ref[...])
        return jnp.dot(high, reduce_ref[...], preferred_element_type=jnp.float32) + jnp.dot(
            low, reduce_ref[...], preferred_element_type=jnp.float32
        )

    def chosen_of(z, y, x):
        chosen = jnp.int32(-1)
        for a in range(AT):
            chosen = jnp.where(owner_ref[z, y, x, a] == me, a, chosen)
        return chosen

    for z in range(size_z):
        for y in range(size_y):
            for x in range(size_x):
                at = (z * size_y + y) * size_x + x
                place = (z * size_x + x) * size_y + y
                chosen = chosen_of(z, y, x)

                @pl.when(chosen < 0)
                def _():
                    op_ref[place] = jnp.zeros(op_ref.shape[1:], op_ref.dtype)

                @pl.when(chosen >= 0)
                def _():
                    shift = (ROWS - 2 * chosen) % ROWS
                    for k in range(9):
                        turned = []
                        for chunk in range(CHUNKS):
                            start = (k * CHUNKS + chunk) * LANES
                            rows = rows_ref[at, :, start : start + LANES].astype(jnp.float32)
                            rows = pltpu.roll(rows, shift, 0)
                            back = chunk * (LANES - GROUP * NV)
                            turned.append(rows if back == 0 else pltpu.roll(rows, LANES - back, 1))
                        for chunk in range(CHUNKS):
                            start = chunk * LANES
                            width = min(LANES, NV * NV - start)
                            value = turned[chunk]
                            if chunk + 1 < CHUNKS:
                                cut = GROUP * NV - chunk * (LANES - GROUP * NV)
                                value = jnp.where(lane8 < cut, value, turned[chunk + 1])
                            op_ref[place, k, :, start : start + width] = value[:2, :width].astype(
                                jnp.bfloat16
                            )

    right_side = rows_ref[:, :, TILES * LANES :].astype(jnp.float32).reshape(count, LANES)
    zero_value = jnp.zeros((1, 1), jnp.float32)

    def squares(value):
        return total(jnp.where(real, value * value, 0.0))

    beta = jnp.sqrt(squares(right_side) + epsilon)
    basis = [right_side / beta]
    swapped = [paired(basis[0])]
    hessen = []
    for row_index in range(ITERS + 1):
        hessen.append([(zero_value, zero_value)] * ITERS)
    for column in range(ITERS):
        work = apply(basis[column], swapped[column])
        for row_index in range(column + 1):
            turned = swapped[row_index] * sign
            coef_re = total(jnp.where(real, basis[row_index] * work, 0.0))
            coef_im = -total(jnp.where(real, turned * work, 0.0))
            hessen[row_index][column] = (coef_re, coef_im)
            work = work - coef_re * basis[row_index] + coef_im * turned
        norm_now = jnp.sqrt(squares(work) + epsilon)
        hessen[column + 1][column] = (norm_now, zero_value)
        if column + 1 < ITERS:
            basis.append(work / norm_now)
            swapped.append(paired(basis[-1]))
    weights = least_squares(hessen, beta)
    answer = jnp.zeros_like(right_side)
    for column in range(ITERS):
        answer = (
            answer
            + weights[column][0] * basis[column]
            - weights[column][1] * (swapped[column] * sign)
        )
    one_ref[...] = answer
    out_ref[...] = jnp.zeros(out_ref.shape, jnp.float32)
    for z in range(size_z):
        for y in range(size_y):
            for x in range(size_x):
                at = (z * size_y + y) * size_x + x
                chosen = chosen_of(z, y, x)
                shift = (ROWS - 2 * jnp.maximum(chosen, 0)) % ROWS
                rows = pltpu.roll(one_ref[at * ROWS : (at + 1) * ROWS], shift, 0)
                rows = jnp.where(chosen >= 0, rows, 0.0)
                place = (z * size_x + x) * size_y + y
                for part in range(2):
                    out_ref[part, place : place + 1] = rows[part : part + 1]
    for part in range(2):
        sol_ref[part] = jnp.transpose(out_ref[part])[:NV, :devices]


def reduce_table():
    table = np.zeros((CHUNKS, LANES, LANES), np.float32)
    for chunk in range(CHUNKS):
        for at in range(GROUP):
            out = chunk * GROUP + at
            if out < NV:
                for copy in range(GROUP):
                    table[chunk, at * NV : (at + 1) * NV, copy * NV + out] = 1.0
    return table.reshape(CHUNKS * LANES, LANES).astype(jnp.bfloat16)


def coarse_solve(rows, owner):
    devices, count = rows.shape[0], rows.shape[0] * ROWS
    vmem = pl.BlockSpec(memory_space=pltpu.VMEM)
    return pl.pallas_call(
        gmres_kernel,
        out_shape=(
            jax.ShapeDtypeStruct((devices, 9, 2, NV * NV), jnp.bfloat16),
            jax.ShapeDtypeStruct((2, NV, devices), jnp.float32),
        ),
        in_specs=[pl.BlockSpec(memory_space=pltpu.SMEM), vmem, vmem],
        out_specs=[vmem, vmem],
        scratch_shapes=[
            pltpu.VMEM((count, CHUNKS * LANES), jnp.float32),
            pltpu.VMEM((count, LANES), jnp.float32),
            pltpu.VMEM((count, LANES), jnp.float32),
            pltpu.VMEM((2, -(-devices // LANES) * LANES, LANES), jnp.float32),
        ],
        compiler_params=pltpu.CompilerParams(vmem_limit_bytes=28 << 20),
    )(owner, rows, reduce_table())


def on_device(vectors, links, site_term, owner, coarse_rhs):
    message = fine_message(
        vectors[0, 0, 0], links[0, 0, 0], site_term[0, 0, 0], coarse_rhs[0, 0, 0]
    )
    rows = gather_messages(message)
    operator, answer = coarse_solve(rows, owner)
    return operator[None], jnp.transpose(answer, (2, 0, 1))[None]


def solution(mesh):
    return jax.shard_map(
        on_device,
        mesh=mesh,
        in_specs=(
            P("gz", "gy", "gx", None, None, None, None, None, None),
            P("gz", "gy", "gx", None, None, None, None, None, None),
            P("gz", "gy", "gx", None, None, None, None, None, None),
            P(),
            P("gz", "gy", "gx", None, None, None),
        ),
        out_specs=(P(("gz", "gx"), None, None, None, None), P(("gz", "gx"), None, None, None)),
        check_vma=False,
    )
```
